256 devices in a mesh: wide: 32 (over x, z), narrow: 8 (over y, core).
Axes of the slice: x: 4, y: 4, z: 8, core: 2. Of those that a mesh axis runs over, the one named last changes fastest.
Arguments:
- coefficients: bfloat16 [4096, 2, 512], P(('wide', 'narrow')), may hold values from -6 to 6
- radiation: bfloat16 [2, 512, 882], replicated, may hold values from -0.1875 to 0.1875
- interpolation: bfloat16 [882, 3328], replicated, may hold values from -0.21875 to 0.21875
- angles: float32 [8, 3328], replicated, may hold values from -3.140625 to 3.140625
- translations: float32 [316, 2, 3328], P(None, None, 'wide'), may hold values from -0.031746034 to 0.031746034
- sources: int32 [512, 189], P(('wide', 'narrow')), may hold values from 0 to 511
- operators: int32 [512, 189], P(('wide', 'narrow')), may hold values from 0 to 315
- counts: int32 [512], P(('wide', 'narrow')), may hold values from 63 to 189, as said below
Outputs:
- product: float32 [4096, 2, 512], P(('wide', 'narrow'))
The draws below stay inside these ranges and needn't reach their ends.
Inputs may be any that keep to these rules, and one draw needn't show every extreme that they name: `counts`: entries of a list past its count are not used; some parent has exactly 189 entries and some exactly 63. `sources`: index values; a program may hold and send them packed several to one 32-bit word, as an allowed encoding. `operators`: index values; a program may hold and send them packed several to one 32-bit word, as an allowed encoding.
All inputs are finite; a program needn't handle non-finite values.
Results may differ from the reference program's by a relative error of at most 0.005.
Values sent between devices are 32-bit elements; how exact they have to be, the bound alone decides.
A program may use at most 128 MiB of HBM per device.

```python
import jax
import jax.numpy as jnp
from jax import lax

NB = 512
Q0 = 882
Q1 = 3328
CH = 8
LIST = 189
OPS = 316
LEAVES = 4096
PARENTS = 512


def draw_counts(key, part):
    values = jax.random.randint(key, (PARENTS,), LIST // 3, LIST + 1)
    values = values.at[0].set(LIST)
    values = values.at[1].set(LIST // 3)
    return values.astype(jnp.int32)


def set_ends(array, key, least, largest):
    spot = [jax.random.randint(jax.random.fold_in(key, axis), (), 0, length) for axis, length in enumerate(array.shape)]
    widest = array.shape.index(max(array.shape))
    beside = spot[:widest] + [(spot[widest] + 1) % array.shape[widest]] + spot[widest + 1:]
    return array.at[tuple(spot)].set(least).at[tuple(beside)].set(largest)


def block_levels(key, shape, pieces, low, high):
    def one(axis_at, shards_of):
        steps = jax.random.uniform(jax.random.fold_in(jax.random.fold_in(key, 6), axis_at), (shards_of,), jnp.float32, low / len(pieces), high / len(pieces))
        return jnp.repeat(jnp.exp(steps), shape[axis_at] // shards_of).reshape((-1,) + (1,) * (len(shape) - axis_at - 1))

    factor_of = one(*pieces[0])
    for cut in pieces[1:]:
        factor_of = factor_of * one(*cut)
    return factor_of


def noise(rng, shape, scale, most, cuts=(), kind=jnp.bfloat16):
    result = scale * jax.random.normal(rng, shape, jnp.float32)
    if cuts:
        result = result * block_levels(rng, shape, cuts, -0.22, 0.18)
    return jnp.clip(result, -most, most).astype(kind)


def setup_inputs(seed: int = 0) -> dict:
    key_list = jax.random.split(jax.random.key(seed), 9)
    coefficients = noise(key_list[0], (LEAVES, 2, NB), 1.0, 6.0, ((0, 256),))
    radiation = noise(key_list[1], (2, NB, Q0), (2 * NB) ** -0.5, 0.1875)
    interpolation = noise(key_list[2], (Q0, Q1), Q0 ** -0.5, 0.21875)
    angles = jnp.clip(jax.random.uniform(key_list[3], (CH, Q1), jnp.float32, -3.140625, 3.140625), -3.140625, 3.140625)
    translations = noise(key_list[4], (OPS, 2, Q1), (1.0 / LIST), 0.031746034, ((2, 32),), jnp.float32)
    sources = set_ends(jax.random.randint(key_list[5], (PARENTS, LIST), 0, PARENTS), jax.random.fold_in(key_list[5], 1), 0, PARENTS - 1).astype(jnp.int32)
    operators = set_ends(jax.random.randint(key_list[6], (PARENTS, LIST), 0, OPS), jax.random.fold_in(key_list[6], 1), 0, OPS - 1).astype(jnp.int32)
    counts = draw_counts(jax.random.fold_in(key_list[8], 71), 0)
    return dict(coefficients=coefficients, radiation=radiation, interpolation=interpolation, angles=angles, translations=translations, sources=sources, operators=operators, counts=counts)


def product_of(left, right):
    return jnp.dot(left, right, preferred_element_type=jnp.float32)


def reference(coefficients, radiation, interpolation, angles, translations, sources, operators, counts):
    coef_real = coefficients[:, 0]
    coef_imag = coefficients[:, 1]
    rad_real = radiation[0]
    rad_imag = radiation[1]
    leaf_real = product_of(coef_real, rad_real) - product_of(coef_imag, rad_imag)
    leaf_imag = product_of(coef_real, rad_imag) + product_of(coef_imag, rad_real)
    leaf = jnp.stack([leaf_real, leaf_imag], 1).astype(jnp.bfloat16)
    upward = product_of(leaf.reshape(LEAVES * 2, Q0), interpolation).reshape(PARENTS, CH, 2, Q1)
    cosines = jnp.cos(angles)[None]
    sines = jnp.sin(angles)[None]
    out_real = jnp.sum(cosines * upward[:, :, 0] - sines * upward[:, :, 1], 1)
    out_imag = jnp.sum(cosines * upward[:, :, 1] + sines * upward[:, :, 0], 1)
    outgoing = jnp.stack([out_real, out_imag], 1)

    def entry_step(carry, column):
        total_real, total_imag = carry
        weight = (column < counts).astype(jnp.float32)[:, None]
        picked = outgoing[sources[:, column]]
        operator_rows = translations[operators[:, column]]
        total_real = total_real + weight * (operator_rows[:, 0] * picked[:, 0] - operator_rows[:, 1] * picked[:, 1])
        total_imag = total_imag + weight * (operator_rows[:, 0] * picked[:, 1] + operator_rows[:, 1] * picked[:, 0])
        return (total_real, total_imag), None

    zeros = jnp.zeros((PARENTS, Q1), jnp.float32)
    (in_real, in_imag), unused = lax.scan(entry_step, (zeros, zeros), jnp.arange(LIST, dtype=jnp.int32))
    down_real = cosines * in_real[:, None] + sines * in_imag[:, None]
    down_imag = cosines * in_imag[:, None] - sines * in_real[:, None]
    downward = jnp.stack([down_real, down_imag], 2).astype(jnp.bfloat16)
    received = lax.dot_general(downward.reshape(LEAVES * 2, Q1), interpolation, (((1,), (1,)), ((), ())), preferred_element_type=jnp.float32)
    received = received.astype(jnp.bfloat16).reshape(LEAVES, 2, Q0)
    dims = (((1,), (1,)), ((), ()))
    recv_real = received[:, 0]
    recv_imag = received[:, 1]
    res_real = lax.dot_general(recv_real, rad_real, dims, preferred_element_type=jnp.float32) + lax.dot_general(recv_imag, rad_imag, dims, preferred_element_type=jnp.float32)
    res_imag = lax.dot_general(recv_imag, rad_real, dims, preferred_element_type=jnp.float32) - lax.dot_general(recv_real, rad_imag, dims, preferred_element_type=jnp.float32)
    return jnp.stack([res_real, res_imag], 1)
```

```python
import functools

import jax
import jax.numpy as jnp
from jax import lax
from jax.experimental import pallas as pl
from jax.experimental.pallas import tpu as pltpu
from jax.sharding import PartitionSpec as P

MESH = pl.DeviceIdType.MESH
BF16 = jnp.bfloat16
F32 = jnp.float32
LANES = 128
GROUP = 8
NO_OPERATOR = 511


def kernel(
    dims,
    counts_ref, coef_ref, rad_hbm, int_hbm, ang_ref, tab_ref, src_ref, opr_ref,
    out_ref,
    rad, itp, cosv, sinv, work, outg, list_send, list_got, x_send, x_got, x_all,
    tab, onehot_x, onehot_t, acc, r_send, r_got, inc, recv_acc,
    mem_sem, list_ss, list_rs, x_ss, x_rs, n_ss, n_rs, r_ss, r_rs,
):
    n_wide, n_narrow, chunk = dims
    me_w = lax.axis_index("wide")
    me_n = lax.axis_index("narrow")
    q0, q1 = int_hbm.shape
    parts = q1 // chunk
    dirs = q1 // n_wide
    n_list = src_ref.shape[1]
    n_rows = 2 * n_wide

    rad_copy = pltpu.make_async_copy(rad_hbm, rad, mem_sem.at[parts])
    rad_copy.start()

    def int_copy(i):
        cols = pl.ds(pl.multiple_of(i * chunk, chunk), chunk)
        return pltpu.make_async_copy(int_hbm.at[:, cols], itp.at[:, cols], mem_sem.at[i])

    lax.fori_loop(0, parts, lambda i, c: (int_copy(i).start(), c)[1], 0)

    barrier = pltpu.get_barrier_semaphore()

    def wide_peer(k):
        return lax.rem(me_w + k, n_wide)

    def narrow_peer(k):
        return lax.rem(me_n + k, n_narrow)

    def greet_wide(k, c):
        pl.semaphore_signal(barrier, 1, device_id=(wide_peer(k), me_n), device_id_type=MESH)
        return c

    def greet_narrow(k, c):
        pl.semaphore_signal(barrier, 1, device_id=(me_w, narrow_peer(k)), device_id_type=MESH)
        return c

    lax.fori_loop(1, n_wide, greet_wide, 0)
    lax.fori_loop(1, n_narrow, greet_narrow, 0)

    src = src_ref[...]
    opr = opr_ref[...]
    half = lax.shift_right_logical(src, 1)
    row = (half % n_narrow) * n_rows + (half // n_narrow) * 2 + (src & 1)
    lane = lax.broadcasted_iota(jnp.int32, src.shape, 1)
    which = lax.broadcasted_iota(jnp.int32, src.shape, 0)
    limit = jnp.where(which == 0, counts_ref[0], counts_ref[1])
    packed = row * 512 + jnp.where(lane < limit, opr, NO_OPERATOR)
    list_send[...] = jnp.full(list_send.shape, NO_OPERATOR, jnp.int32)
    list_send[:, pl.ds(0, n_list)] = packed

    work_t = jnp.zeros((2 * LANES, tab.shape[0]), F32)
    n_ops = tab_ref.shape[2]
    for c in range(2):
        t = tab_ref[c]
        t = jnp.concatenate([t, jnp.zeros((LANES - dirs, n_ops), F32)], 0)
        t = jnp.concatenate([t, jnp.zeros((LANES, tab.shape[0] - n_ops), F32)], 1)
        tab[:, pl.ds(c * LANES, LANES)] = t.T.astype(BF16)

    rad_copy.wait()
    half_rows = coef_ref.shape[0] // 2
    work[...] = lax.dot_general(
        rad[...], coef_ref[...], (((1,), (1,)), ((), ())), preferred_element_type=F32
    )
    by_real = work[pl.ds(0, q0, stride=2), :]
    by_imag = work[pl.ds(1, q0, stride=2), :]
    leaf_t = jnp.concatenate(
        [
            by_real[:, :half_rows] - by_imag[:, half_rows:],
            by_imag[:, :half_rows] + by_real[:, half_rows:],
        ],
        1,
    )
    leaf = leaf_t.T.astype(BF16)

    def up_chunk(i, c):
        cols = pl.ds(pl.multiple_of(i * chunk, chunk), chunk)
        ang = ang_ref[:, cols]
        co = jnp.cos(ang)
        si = jnp.sin(ang)
        cosv[:, cols] = co
        sinv[:, cols] = si
        int_copy(i).wait()
        up = jnp.dot(leaf, itp[:, cols], preferred_element_type=F32)
        for p in range(2):
            ur = up[8 * p : 8 * p + 8]
            ui = up[16 + 8 * p : 24 + 8 * p]
            outg[pl.ds(p, 1), cols] = jnp.sum(co * ur - si * ui, 0, keepdims=True)
            outg[pl.ds(2 + p, 1), cols] = jnp.sum(co * ui + si * ur, 0, keepdims=True)
        return c

    lax.fori_loop(0, parts, up_chunk, 0)

    pl.semaphore_wait(barrier, n_wide - 1 + n_narrow - 1)

    def list_out(k):
        return pltpu.make_async_remote_copy(
            src_ref=list_send, dst_ref=list_got.at[me_w], send_sem=list_ss.at[k],
            recv_sem=list_rs.at[me_w], device_id=(wide_peer(k), me_n), device_id_type=MESH)

    def list_in(k):
        w = wide_peer(k)
        return pltpu.make_async_remote_copy(
            src_ref=list_send, dst_ref=list_got.at[w], send_sem=list_ss.at[k],
            recv_sem=list_rs.at[w], device_id=(w, me_n), device_id_type=MESH)

    for w in range(n_wide):
        tile, off = divmod(w * dirs, LANES)
        piece = outg[:, pl.ds(tile * LANES, LANES)]
        if off:
            piece = pltpu.roll(piece, LANES - off, 1)
            if off + dirs > LANES:
                more = pltpu.roll(outg[:, pl.ds((tile + 1) * LANES, LANES)], LANES - off, 1)
                at = lax.broadcasted_iota(jnp.int32, piece.shape, 1)
                piece = jnp.where(at < LANES - off, piece, more)
        x_send[w, :, pl.ds(0, LANES)] = piece[0:2]
        x_send[w, :, pl.ds(LANES, LANES)] = piece[2:4]

    def x_out(k):
        w = wide_peer(k)
        return pltpu.make_async_remote_copy(
            src_ref=x_send.at[w], dst_ref=x_got.at[me_w], send_sem=x_ss.at[k],
            recv_sem=x_rs.at[me_w], device_id=(w, me_n), device_id_type=MESH)

    def x_in(k):
        w = wide_peer(k)
        return pltpu.make_async_remote_copy(
            src_ref=x_send.at[w], dst_ref=x_got.at[w], send_sem=x_ss.at[k],
            recv_sem=x_rs.at[w], device_id=(w, me_n), device_id_type=MESH)

    def start(make):
        return lambda k, c: (make(k).start(), c)[1]

    def got(make):
        return lambda k, c: (make(k).wait_recv(), c)[1]

    def sent(make):
        return lambda k, c: (make(k).wait_send(), c)[1]

    lax.fori_loop(1, n_wide, start(x_out), 0)
    lax.fori_loop(1, n_wide, start(list_out), 0)
    x_got[me_w] = x_send[me_w]
    list_got[me_w] = list_send[...]
    lax.fori_loop(1, n_wide, got(x_in), 0)
    x_all[me_n] = x_got[...].reshape(n_rows, 2 * LANES)

    def n_out(k):
        return pltpu.make_async_remote_copy(
            src_ref=x_all.at[me_n], dst_ref=x_all.at[me_n], send_sem=n_ss.at[k],
            recv_sem=n_rs.at[me_n], device_id=(me_w, narrow_peer(k)), device_id_type=MESH)

    def n_in(k):
        n = narrow_peer(k)
        return pltpu.make_async_remote_copy(
            src_ref=x_all.at[me_n], dst_ref=x_all.at[n], send_sem=n_ss.at[k],
            recv_sem=n_rs.at[n], device_id=(me_w, n), device_id_type=MESH)

    lax.fori_loop(1, n_narrow, start(n_out), 0)
    lax.fori_loop(1, n_wide, got(list_in), 0)
    lists = list_got[...]
    lists = [lists[:, :, t * LANES : (t + 1) * LANES].reshape(n_rows, LANES) for t in range(2)]
    lax.fori_loop(1, n_narrow, got(n_in), 0)
    rows_all = n_narrow * n_rows
    pat = x_all[...].astype(BF16).reshape(rows_all, 2 * LANES)

    acc[...] = jnp.zeros(acc.shape, F32)
    at_x = lax.broadcasted_iota(jnp.int32, (n_rows, rows_all), 1)
    at_t = lax.broadcasted_iota(jnp.int32, (n_rows, tab.shape[0]), 1)
    for t in range(2):
        held = lists[t]
        steps = -(-min(n_list - t * LANES, LANES) // GROUP)

        def step(i, c, held=held):
            here = pltpu.roll(held, lax.rem(LANES - i * GROUP, LANES), 1)
            for u in range(GROUP):
                entry = here[:, u : u + 1]
                source = lax.shift_right_logical(entry, 9)
                oper = entry & 511
                rows = pl.ds(u * n_rows, n_rows)
                onehot_x[rows, :] = jnp.where(source == at_x, 1.0, 0.0).astype(BF16)
                onehot_t[rows, :] = jnp.where(oper == at_t, 1.0, 0.0).astype(BF16)
            px = jnp.dot(onehot_x[...], pat, preferred_element_type=F32)
            pt = jnp.dot(onehot_t[...], tab[...], preferred_element_type=F32)
            xr, xi = px[:, :LANES], px[:, LANES:]
            tr, ti = pt[:, :LANES], pt[:, LANES:]
            real = (tr * xr - ti * xi).reshape(GROUP, n_rows, LANES).sum(0)
            imag = (tr * xi + ti * xr).reshape(GROUP, n_rows, LANES).sum(0)
            acc[:, pl.ds(0, LANES)] += real
            acc[:, pl.ds(LANES, LANES)] += imag
            return c

        lax.fori_loop(0, steps, step, 0)

    r_send[...] = acc[...].reshape(n_wide, 2, 2 * LANES)

    def r_out(k):
        w = wide_peer(k)
        return pltpu.make_async_remote_copy(
            src_ref=r_send.at[w], dst_ref=r_got.at[me_w], send_sem=r_ss.at[k],
            recv_sem=r_rs.at[me_w], device_id=(w, me_n), device_id_type=MESH)

    def r_in(k):
        w = wide_peer(k)
        return pltpu.make_async_remote_copy(
            src_ref=r_send.at[w], dst_ref=r_got.at[w], send_sem=r_ss.at[k],
            recv_sem=r_rs.at[w], device_id=(w, me_n), device_id_type=MESH)

    lax.fori_loop(1, n_wide, start(r_out), 0)
    r_got[me_w] = r_send[me_w]
    recv_acc[...] = jnp.zeros(recv_acc.shape, F32)
    lax.fori_loop(1, n_wide, got(r_in), 0)

    tiles = [None] * (q1 // LANES)
    at = lax.broadcasted_iota(jnp.int32, (4, LANES), 1)
    for w in range(n_wide):
        tile, off = divmod(w * dirs, LANES)
        piece = jnp.concatenate(
            [r_got[w, :, pl.ds(0, LANES)], r_got[w, :, pl.ds(LANES, LANES)]], 0
        )
        if off:
            piece = pltpu.roll(piece, off, 1)
        if tiles[tile] is None:
            tiles[tile] = piece
        else:
            tiles[tile] = jnp.where(at < off, tiles[tile], piece)
        if off + dirs > LANES:
            tiles[tile + 1] = piece
    for i, tile in enumerate(tiles):
        inc[:, pl.ds(i * LANES, LANES)] = tile

    def down_chunk(i, c):
        cols = pl.ds(pl.multiple_of(i * chunk, chunk), chunk)
        co = cosv[:, cols]
        si = sinv[:, cols]
        real, imag = [], []
        for p in range(2):
            ir = inc[pl.ds(p, 1), cols]
            ii = inc[pl.ds(2 + p, 1), cols]
            real.append(co * ir + si * ii)
            imag.append(co * ii - si * ir)
        down = jnp.concatenate(real + imag, 0).astype(BF16)
        recv_acc[...] += lax.dot_general(
            itp[:, cols], down, (((1,), (1,)), ((), ())), preferred_element_type=F32
        )
        return c

    lax.fori_loop(0, parts, down_chunk, 0)

    got_t = recv_acc[...]
    work[pl.ds(0, q0, stride=2), :] = got_t
    work[pl.ds(1, q0, stride=2), :] = jnp.concatenate(
        [got_t[:, half_rows:], -got_t[:, :half_rows]], 1
    )
    out_ref[...] = jnp.dot(
        work[...].T.astype(BF16), rad[...], preferred_element_type=F32
    )

    for make in (list_out, x_out, r_out):
        lax.fori_loop(1, n_wide, sent(make), 0)
    lax.fori_loop(1, n_narrow, sent(n_out), 0)


def solution(mesh):
    n_wide, n_narrow = mesh.shape["wide"], mesh.shape["narrow"]
    both = ("wide", "narrow")

    def on_device(coef, rad, interp, angles, table, sources, operators, counts):
        boxes, _, n_bases = coef.shape
        q0, q1 = interp.shape
        n_ops = table.shape[0]
        chunk = 256 if q1 % 256 == 0 else 128
        parts = q1 // chunk
        rows = 2 * n_wide
        coef_rows = jnp.transpose(coef, (1, 0, 2)).reshape(2 * boxes, n_bases)
        rad_rows = jnp.transpose(rad, (2, 0, 1)).reshape(2 * q0, n_bases)
        table_t = jnp.transpose(table, (1, 2, 0))
        n_tab = -(-n_ops // LANES) * LANES
        vmem = pl.BlockSpec(memory_space=pltpu.VMEM)
        anyw = pl.BlockSpec(memory_space=pl.ANY)
        smem = pl.BlockSpec(memory_space=pltpu.SMEM)
        dma = pltpu.SemaphoreType.DMA
        result = pl.pallas_call(
            functools.partial(kernel, (n_wide, n_narrow, chunk)),
            out_shape=jax.ShapeDtypeStruct((2 * boxes, n_bases), F32),
            in_specs=[smem, vmem, anyw, anyw, vmem, vmem, vmem, vmem],
            out_specs=vmem,
            scratch_shapes=[
                pltpu.VMEM((2 * q0, n_bases), BF16),
                pltpu.VMEM((q0, q1), BF16),
                pltpu.VMEM((8, q1), F32),
                pltpu.VMEM((8, q1), F32),
                pltpu.VMEM((2 * q0, 2 * boxes), F32),
                pltpu.VMEM((4, q1), F32),
                pltpu.VMEM((2, 2 * LANES), jnp.int32),
                pltpu.VMEM((n_wide, 2, 2 * LANES), jnp.int32),
                pltpu.VMEM((n_wide, 2, 2 * LANES), F32),
                pltpu.VMEM((n_wide, 2, 2 * LANES), F32),
                pltpu.VMEM((n_narrow, rows, 2 * LANES), F32),
                pltpu.VMEM((n_tab, 2 * LANES), BF16),
                pltpu.VMEM((GROUP * rows, n_narrow * rows), BF16),
                pltpu.VMEM((GROUP * rows, n_tab), BF16),
                pltpu.VMEM((rows, 2 * LANES), F32),
                pltpu.VMEM((n_wide, 2, 2 * LANES), F32),
                pltpu.VMEM((n_wide, 2, 2 * LANES), F32),
                pltpu.VMEM((4, q1), F32),
                pltpu.VMEM((q0, 2 * boxes), F32),
                dma((parts + 1,)),
                dma((n_wide,)), dma((n_wide,)),
                dma((n_wide,)), dma((n_wide,)),
                dma((n_narrow,)), dma((n_narrow,)),
                dma((n_wide,)), dma((n_wide,)),
            ],
            compiler_params=pltpu.CompilerParams(
                collective_id=0, has_side_effects=True, vmem_limit_bytes=40 << 20
            ),
            name="fmm_step",
        )(counts, coef_rows, rad_rows, interp, angles, table_t, sources, operators)
        return jnp.transpose(result.reshape(2, boxes, n_bases), (1, 0, 2))

    return jax.shard_map(
        on_device,
        mesh=mesh,
        in_specs=(
            P(both, None, None), P(), P(), P(), P(None, None, "wide"),
            P(both, None), P(both, None), P(both),
        ),
        out_specs=P(both, None, None),
        check_vma=False,
    )
```

```python
import functools

import jax
import jax.numpy as jnp
from jax import lax
from jax.experimental import pallas as pl
from jax.experimental.pallas import tpu as pltpu
from jax.sharding import PartitionSpec as P

MESH = pl.DeviceIdType.MESH
BF16 = jnp.bfloat16
F32 = jnp.float32
LANES = 128
GROUP = 32
HALVES = 2
NO_OPERATOR = 511


def offsets_along(n_x, n_z):
    def hops(o):
        return min(o[0], n_x - o[0]) + min(o[1], n_z - o[1])

    return sorted(((a, b) for a in range(n_x) for b in range(n_z)), key=lambda o: (-hops(o), o))


def kernel(
    dims,
    counts_ref, coef_ref, rad_hbm, int_hbm, ang_ref, tab_ref, src_ref, opr_ref,
    out_ref,
    raw, rad, itp, cosv, sinv, work, coefs, outg, list_send, list_got, lists, x_send, x_got, x_all,
    tab, picks, r_send, r_got, inc, recv_acc,
    mem_sem, list_ss, list_rs, x_ss, x_rs, n_ss, n_rs, r_ss, r_rs,
):
    n_wide, n_narrow, n_z, chunk = dims
    n_x = n_wide // n_z
    me_w = lax.axis_index("wide")
    me_n = lax.axis_index("narrow")
    me_x, me_z = me_w // n_z, me_w % n_z
    q0, q1 = int_hbm.shape
    parts = q1 // chunk
    dirs = q1 // n_wide
    n_list = src_ref.shape[1]
    n_rows = 2 * n_wide
    per_half = n_rows // HALVES
    per_tile = LANES // GROUP
    steps = -(-n_list // GROUP)
    boxes = coef_ref.shape[0]

    rad_copy = pltpu.make_async_copy(rad_hbm, raw, mem_sem.at[parts])
    rad_copy.start()

    def int_copy(i):
        cols = pl.ds(i * chunk, chunk)
        return pltpu.make_async_copy(int_hbm.at[:, cols], itp.at[:, cols], mem_sem.at[i])

    for i in range(parts):
        int_copy(i).start()

    barrier = pltpu.get_barrier_semaphore()
    offsets = offsets_along(n_x, n_z)
    place = {o: i for i, o in enumerate(offsets)}
    peers = []
    for dx, dz in offsets:
        w = lax.rem(me_x + dx, n_x) * n_z + lax.rem(me_z + dz, n_z)
        peers.append((w, place[(-dx) % n_x, (-dz) % n_z]))
    for w, _ in peers[:-1]:
        pl.semaphore_signal(barrier, 1, device_id=(w, me_n), device_id_type=MESH)
    me_y, me_c = me_n // 2, me_n % 2
    n_y = n_narrow // 2
    ahead = 1 - 2 * me_c
    n_up = lax.rem(me_y + ahead + n_y, n_y) * 2 + me_c
    n_dn = lax.rem(me_y - ahead + n_y, n_y) * 2 + me_c
    n_far = lax.rem(me_y + 2, n_y) * 2 + me_c
    n_par = me_y * 2 + 1 - me_c
    for n in (n_up, n_dn, n_par):
        pl.semaphore_signal(barrier, 1, device_id=(me_w, n), device_id_type=MESH)

    src = src_ref[...]
    opr = opr_ref[...]
    half = lax.shift_right_logical(src, 1)
    row = (half % n_narrow) * n_rows + (half // n_narrow) * 2 + (src & 1)
    lane = lax.broadcasted_iota(jnp.int32, src.shape, 1)
    which = lax.broadcasted_iota(jnp.int32, src.shape, 0)
    limit = jnp.where(which == 0, counts_ref[0], counts_ref[1])
    packed = row * 512 + jnp.where(lane < limit, opr, NO_OPERATOR)
    list_send[...] = jnp.full(list_send.shape, NO_OPERATOR, jnp.int32)
    list_send[:, pl.ds(0, n_list)] = packed

    n_ops = tab_ref.shape[2]
    for c in range(2):
        t = tab_ref[c]
        t = jnp.concatenate([t, jnp.zeros((LANES - dirs, n_ops), F32)], 0)
        t = jnp.concatenate([t, jnp.zeros((LANES, tab.shape[0] - n_ops), F32)], 1)
        tab[:, pl.ds(c * LANES, LANES)] = t.T.astype(BF16)

    tiled = coef_ref[...].astype(F32).reshape(2 * boxes, -1)
    bases = range(coefs.shape[0])
    for t in bases:
        coefs[t] = tiled[:, t * LANES : (t + 1) * LANES]
    coef = jnp.concatenate(
        [
            jnp.concatenate([coefs[t, pl.ds(c, boxes, stride=2), :] for t in bases], 1)
            for c in range(2)
        ],
        0,
    ).astype(BF16)

    rad_copy.wait()
    rad[...] = raw[...].reshape(rad.shape)
    work[...] = lax.dot_general(
        rad[...], coef, (((1,), (1,)), ((), ())), preferred_element_type=F32
    )
    by_real = work[pl.ds(0, q0, stride=2), :]
    by_imag = work[pl.ds(1, q0, stride=2), :]
    leaf_t = jnp.concatenate(
        [by_real[:, :boxes] - by_imag[:, boxes:], by_imag[:, :boxes] + by_real[:, boxes:]], 1
    )
    leaf = leaf_t.T.astype(BF16)

    def up_chunk(i):
        cols = pl.ds(i * chunk, chunk)
        ang = ang_ref[:, cols]
        co = jnp.cos(ang)
        si = jnp.sin(ang)
        cosv[:, cols] = co
        sinv[:, cols] = si
        int_copy(i).wait()
        up = jnp.dot(leaf, itp[:, cols], preferred_element_type=F32)
        for p in range(2):
            ur = up[8 * p : 8 * p + 8]
            ui = up[boxes + 8 * p : boxes + 8 * p + 8]
            outg[pl.ds(p, 1), cols] = jnp.sum(co * ur - si * ui, 0, keepdims=True)
            outg[pl.ds(2 + p, 1), cols] = jnp.sum(co * ui + si * ur, 0, keepdims=True)

    early = parts * 3 // 4
    for i in range(early):
        up_chunk(i)

    pl.semaphore_wait(barrier, n_wide - 1 + 3)

    def list_copy(w, there):
        return pltpu.make_async_remote_copy(
            src_ref=list_send, dst_ref=list_got.at[there], send_sem=list_ss, recv_sem=list_rs,
            device_id=(w, me_n), device_id_type=MESH)

    for w, there in peers[:-1]:
        list_copy(w, there).start()
    list_got[n_wide - 1] = list_send[...]

    for i in range(early, parts):
        up_chunk(i)

    for w in range(n_wide):
        tile, off = divmod(w * dirs, LANES)
        piece = outg[:, pl.ds(tile * LANES, LANES)]
        if off:
            piece = pltpu.roll(piece, LANES - off, 1)
            if off + dirs > LANES:
                more = pltpu.roll(outg[:, pl.ds((tile + 1) * LANES, LANES)], LANES - off, 1)
                at = lax.broadcasted_iota(jnp.int32, piece.shape, 1)
                piece = jnp.where(at < LANES - off, piece, more)
        x_send[w, :, pl.ds(0, LANES)] = piece[0:2]
        x_send[w, :, pl.ds(LANES, LANES)] = piece[2:4]

    def slice_copy(src_all, dst_all, at, w, send_sem, recv_sem):
        return pltpu.make_async_remote_copy(
            src_ref=src_all.at[at], dst_ref=dst_all.at[me_w], send_sem=send_sem,
            recv_sem=recv_sem, device_id=(w, me_n), device_id_type=MESH)

    def all_of(src_all, dst_all, send_sem, recv_sem):
        most = pl.ds(0, n_wide - 1)
        return pltpu.make_async_remote_copy(
            src_ref=src_all.at[most], dst_ref=dst_all.at[most], send_sem=send_sem,
            recv_sem=recv_sem, device_id=(peers[0][0], me_n), device_id_type=MESH)

    for w, _ in peers[:-1]:
        slice_copy(x_send, x_got, w, w, x_ss, x_rs).start()
    x_got[me_w] = x_send[me_w]

    all_of(list_got, list_got, list_ss, list_rs).wait_recv()
    for h in range(HALVES):
        mine = slice(h * n_wide // HALVES, (h + 1) * n_wide // HALVES)
        for t in range(2):
            lists[h, t] = list_got[mine, :, t * LANES : (t + 1) * LANES].reshape(per_half, LANES)

    def entries(g):
        s = g % steps
        held = lists[g // steps, s // per_tile]
        here = pltpu.roll(held, lax.rem(LANES - s % per_tile * GROUP, LANES), 1)
        columns = [here[:, u : u + 1] for u in range(GROUP)]
        return jnp.concatenate([jnp.broadcast_to(c, (per_half, LANES)) for c in columns], 0)

    lane_at = lax.broadcasted_iota(jnp.int32, (GROUP * per_half, LANES), 1)

    def one_hot(index, n):
        tiles = [jnp.where(index == lane_at + t, 1.0, 0.0).astype(BF16) for t in range(0, n, LANES)]
        return jnp.concatenate(tiles, 1)

    def pick_operators(g, c):
        onehot = one_hot(entries(g) & 511, tab.shape[0])
        picks[g] = jnp.dot(onehot, tab[...], preferred_element_type=F32).astype(BF16)
        return c

    total = HALVES * steps
    cuts = [0, total // 6, total * 7 // 12, total]
    lax.fori_loop(cuts[0], cuts[1], pick_operators, 0)

    all_of(x_got, x_got, x_ss, x_rs).wait_recv()
    x_all[me_n] = x_got[...].reshape(n_rows, 2 * LANES)

    def block_copy(k, block, to):
        return pltpu.make_async_remote_copy(
            src_ref=x_all.at[block], dst_ref=x_all.at[block], send_sem=n_ss.at[k],
            recv_sem=n_rs.at[block], device_id=(me_w, to), device_id_type=MESH)

    moves = [
        block_copy(0, me_n, n_up), block_copy(1, me_n, n_dn), block_copy(2, me_n, n_par),
        block_copy(3, n_dn, n_up), block_copy(4, n_dn, n_par), block_copy(5, n_up, n_par),
        block_copy(6, n_far, n_par),
    ]
    for m in moves[:3]:
        m.start()
    lax.fori_loop(cuts[1], cuts[2], pick_operators, 0)
    block_copy(0, n_dn, n_up).wait_recv()
    moves[3].start()
    moves[4].start()
    block_copy(0, n_up, n_up).wait_recv()
    moves[5].start()
    lax.fori_loop(cuts[2], cuts[3], pick_operators, 0)
    block_copy(0, n_far, n_up).wait_recv()
    moves[6].start()
    for y in range(n_y):
        block_copy(0, y * 2 + 1 - me_c, n_par).wait_recv()
    rows_all = n_narrow * n_rows
    pat = x_all[...].astype(BF16).reshape(rows_all, 2 * LANES)

    def translate(g, c):
        onehot = one_hot(lax.shift_right_logical(entries(g), 9), rows_all)
        px = jnp.dot(onehot, pat, preferred_element_type=F32)
        pt = picks[g].astype(F32)
        xr, xi = px[:, :LANES], px[:, LANES:]
        tr, ti = pt[:, :LANES], pt[:, LANES:]
        real = (tr * xr - ti * xi).reshape(GROUP, per_half, LANES).sum(0)
        imag = (tr * xi + ti * xr).reshape(GROUP, per_half, LANES).sum(0)
        return c[0] + real, c[1] + imag

    for h in range(HALVES):
        zero = jnp.zeros((per_half, LANES), F32)
        real, imag = lax.fori_loop(h * steps, (h + 1) * steps, translate, (zero, zero))
        mine = slice(h * n_wide // HALVES, (h + 1) * n_wide // HALVES)
        r_send[mine, :, pl.ds(0, LANES)] = real.reshape(-1, 2, LANES)
        r_send[mine, :, pl.ds(LANES, LANES)] = imag.reshape(-1, 2, LANES)
        for i in range(mine.start, min(mine.stop, n_wide - 1)):
            slice_copy(r_send, r_got, i, peers[i][0], r_ss, r_rs).start()
    r_got[me_w] = r_send[n_wide - 1]
    recv_acc[...] = jnp.zeros(recv_acc.shape, F32)
    all_of(r_got, r_got, r_ss, r_rs).wait_recv()

    tiles = [None] * (q1 // LANES)
    at = lax.broadcasted_iota(jnp.int32, (4, LANES), 1)
    for w in range(n_wide):
        tile, off = divmod(w * dirs, LANES)
        piece = jnp.concatenate(
            [r_got[w, :, pl.ds(0, LANES)], r_got[w, :, pl.ds(LANES, LANES)]], 0
        )
        if off:
            piece = pltpu.roll(piece, off, 1)
        if tiles[tile] is None:
            tiles[tile] = piece
        else:
            tiles[tile] = jnp.where(at < off, tiles[tile], piece)
        if off + dirs > LANES:
            tiles[tile + 1] = piece
    for i, tile in enumerate(tiles):
        inc[:, pl.ds(i * LANES, LANES)] = tile

    def down_chunk(i, c):
        cols = pl.ds(pl.multiple_of(i * chunk, chunk), chunk)
        co = cosv[:, cols]
        si = sinv[:, cols]
        real, imag = [], []
        for p in range(2):
            ir = inc[pl.ds(p, 1), cols]
            ii = inc[pl.ds(2 + p, 1), cols]
            real.append(co * ir + si * ii)
            imag.append(co * ii - si * ir)
        down = jnp.concatenate(real + imag, 0).astype(BF16)
        recv_acc[...] += lax.dot_general(
            itp[:, cols], down, (((1,), (1,)), ((), ())), preferred_element_type=F32
        )
        return c

    lax.fori_loop(0, parts, down_chunk, 0)

    got_t = recv_acc[...]
    work[pl.ds(0, q0, stride=2), :] = got_t
    work[pl.ds(1, q0, stride=2), :] = jnp.concatenate([got_t[:, boxes:], -got_t[:, :boxes]], 1)
    result = jnp.dot(work[...].T.astype(BF16), rad[...], preferred_element_type=F32)
    for t in bases:
        cols = slice(t * LANES, (t + 1) * LANES)
        coefs[t, pl.ds(0, boxes, stride=2), :] = result[:boxes, cols]
        coefs[t, pl.ds(1, boxes, stride=2), :] = result[boxes:, cols]
        out_ref[:, :, pl.ds(t * LANES, LANES)] = coefs[t].reshape(boxes, 2, LANES)

    all_of(list_got, list_got, list_ss, list_rs).wait_send()
    all_of(x_send, x_got, x_ss, x_rs).wait_send()
    all_of(r_send, r_got, r_ss, r_rs).wait_send()
    for m in moves:
        m.wait_send()


def solution(mesh):
    n_wide, n_narrow = mesh.shape["wide"], mesh.shape["narrow"]
    n_z = 8
    both = ("wide", "narrow")

    def on_device(coef, rad, interp, angles, table, sources, operators, counts):
        boxes, _, n_bases = coef.shape
        q0, q1 = interp.shape
        n_ops = table.shape[0]
        n_list = sources.shape[1]
        chunk = 256
        parts = q1 // chunk
        rows = 2 * n_wide
        rad_raw = jnp.transpose(rad, (2, 0, 1))
        table_t = jnp.transpose(table, (1, 2, 0))
        n_tab = -(-n_ops // LANES) * LANES
        steps = -(-n_list // GROUP)
        vmem = pl.BlockSpec(memory_space=pltpu.VMEM)
        anyw = pl.BlockSpec(memory_space=pl.ANY)
        smem = pl.BlockSpec(memory_space=pltpu.SMEM)
        dma = pltpu.SemaphoreType.DMA
        slots = (n_wide, 2, 2 * LANES)
        return pl.pallas_call(
            functools.partial(kernel, (n_wide, n_narrow, n_z, chunk)),
            out_shape=jax.ShapeDtypeStruct((boxes, 2, n_bases), F32),
            in_specs=[smem, vmem, anyw, anyw, vmem, vmem, vmem, vmem],
            out_specs=vmem,
            scratch_shapes=[
                pltpu.VMEM((q0, 2, n_bases), BF16),
                pltpu.VMEM((2 * q0, n_bases), BF16),
                pltpu.VMEM((q0, q1), BF16),
                pltpu.VMEM((8, q1), F32),
                pltpu.VMEM((8, q1), F32),
                pltpu.VMEM((2 * q0, 2 * boxes), F32),
                pltpu.VMEM((n_bases // LANES, 2 * boxes, LANES), F32),
                pltpu.VMEM((4, q1), F32),
                pltpu.VMEM((2, 2 * LANES), jnp.int32),
                pltpu.VMEM(slots, jnp.int32),
                pltpu.VMEM((HALVES, 2, rows // HALVES, LANES), jnp.int32),
                pltpu.VMEM(slots, F32),
                pltpu.VMEM(slots, F32),
                pltpu.VMEM((n_narrow, rows, 2 * LANES), F32),
                pltpu.VMEM((n_tab, 2 * LANES), BF16),
                pltpu.VMEM((HALVES * steps, GROUP * rows // HALVES, 2 * LANES), BF16),
                pltpu.VMEM(slots, F32),
                pltpu.VMEM(slots, F32),
                pltpu.VMEM((4, q1), F32),
                pltpu.VMEM((q0, 2 * boxes), F32),
                dma((parts + 1,)),
                dma, dma, dma, dma, dma((7,)), dma((n_narrow,)), dma, dma,
            ],
            compiler_params=pltpu.CompilerParams(
                collective_id=0, has_side_effects=True, vmem_limit_bytes=60 * 1024 * 1024
            ),
            name="fmm_step",
        )(counts, coef, rad_raw, interp, angles, table_t, sources, operators)

    return jax.shard_map(
        on_device,
        mesh=mesh,
        in_specs=(
            P(both, None, None), P(), P(), P(), P(None, None, "wide"),
            P(both, None), P(both, None), P(both),
        ),
        out_specs=P(both, None, None),
        check_vma=False,
    )
```

```python
import functools

import jax
import jax.numpy as jnp
from jax import lax
from jax.experimental import pallas as pl
from jax.experimental.pallas import tpu as pltpu
from jax.sharding import PartitionSpec as P

MESH = pl.DeviceIdType.MESH
BF16 = jnp.bfloat16
F32 = jnp.float32
LANES = 128
GROUP = 96
STEPS = 2
SHARES = 4
CHUNKS = 2
NO_OPERATOR = 511


def offsets_along(n_x, n_z):
    def hops(o):
        return min(o[0], n_x - o[0]) + min(o[1], n_z - o[1])

    return sorted(((a, b) for a in range(n_x) for b in range(n_z)), key=lambda o: (-hops(o), o))


def kernel(
    dims,
    counts_hbm, coef_hbm, rad_hbm, int_hbm, ang_hbm, tab_hbm, src_hbm, opr_hbm,
    out_ref,
    counts_ref, coef_ref, ang_ref, tab_ref, src_ref, opr_ref,
    raw, rad, itp, cosv, sinv, work, coefs, outg, list_send, list_got, lists, x_send, x_got, x_all,
    tab, picks, down, r_send, r_got, inc, recv_acc,
    mem_sem, list_ss, list_rs, x_ss, x_rs, n_ss, n_rs, r_ss, r_rs,
):
    n_wide, n_narrow, n_z, chunk = dims
    n_x = n_wide // n_z
    me_w = lax.axis_index("wide")
    me_n = lax.axis_index("narrow")
    me_x, me_z = me_w // n_z, me_w % n_z
    q0, q1 = int_hbm.shape
    parts = q1 // chunk
    dirs = q1 // n_wide
    n_list = src_ref.shape[1]
    n_rows = 2 * n_wide
    per_share = n_rows // SHARES
    per_chunk = n_wide // CHUNKS
    boxes = coef_ref.shape[0]

    small = [
        pltpu.make_async_copy(a, b, mem_sem.at[parts + 1 + i])
        for i, (a, b) in enumerate([
            (ang_hbm, ang_ref), (coef_hbm, coef_ref), (src_hbm, src_ref), (opr_hbm, opr_ref),
            (counts_hbm, counts_ref), (tab_hbm, tab_ref),
        ])
    ]
    small[0].start()
    rad_copy = pltpu.make_async_copy(rad_hbm, raw, mem_sem.at[parts])
    rad_copy.start()
    for copy in small[1:]:
        copy.start()

    def int_copy(i):
        cols = pl.ds(i * chunk, chunk)
        return pltpu.make_async_copy(int_hbm.at[:, cols], itp.at[:, cols], mem_sem.at[i])

    for i in range(parts):
        int_copy(i).start()

    barrier = pltpu.get_barrier_semaphore()
    offsets = offsets_along(n_x, n_z)
    place = {o: i for i, o in enumerate(offsets)}
    peers = []
    for dx, dz in offsets:
        w = lax.rem(me_x + dx, n_x) * n_z + lax.rem(me_z + dz, n_z)
        peers.append((w, place[(-dx) % n_x, (-dz) % n_z]))
    for w, _ in peers[:-1]:
        pl.semaphore_signal(barrier, 1, device_id=(w, me_n), device_id_type=MESH)
    me_y, me_c = me_n // 2, me_n % 2
    n_y = n_narrow // 2
    ahead = 1 - 2 * me_c
    n_up = lax.rem(me_y + ahead + n_y, n_y) * 2 + me_c
    n_dn = lax.rem(me_y - ahead + n_y, n_y) * 2 + me_c
    n_far = lax.rem(me_y + 2, n_y) * 2 + me_c
    n_par = me_y * 2 + 1 - me_c
    n_cross = n_up + ahead
    for n in (n_up, n_dn, n_par, n_cross):
        pl.semaphore_signal(barrier, 1, device_id=(me_w, n), device_id_type=MESH)

    small[0].wait()
    for i in range(parts):
        cols = pl.ds(i * chunk, chunk)
        cosv[:, cols] = jnp.cos(ang_ref[:, cols])
        sinv[:, cols] = jnp.sin(ang_ref[:, cols])

    for copy in small[1:]:
        copy.wait()
    src = src_ref[...]
    opr = opr_ref[...]
    half = lax.shift_right_logical(src, 1)
    row = (half % n_narrow) * n_rows + (half // n_narrow) * 2 + (src & 1)
    lane = lax.broadcasted_iota(jnp.int32, src.shape, 1)
    which = lax.broadcasted_iota(jnp.int32, src.shape, 0)
    limit = jnp.where(which == 0, counts_ref[0], counts_ref[1])
    packed = row * 512 + jnp.where(lane < limit, opr, NO_OPERATOR)
    list_send[...] = jnp.full(list_send.shape, NO_OPERATOR, jnp.int32)
    list_send[:, pl.ds(0, GROUP)] = packed[:, :GROUP]
    list_send[:, pl.ds(LANES, n_list - GROUP)] = packed[:, GROUP:]

    n_ops = tab_ref.shape[2]
    for c in range(2):
        t = tab_ref[c]
        t = jnp.concatenate([t, jnp.zeros((LANES - dirs, n_ops), F32)], 0)
        t = jnp.concatenate([t, jnp.zeros((LANES, tab.shape[0] - n_ops), F32)], 1)
        tab[:, pl.ds(c * LANES, LANES)] = t.T.astype(BF16)

    tiled = coef_ref[...].astype(F32).reshape(2 * boxes, -1)
    bases = range(coefs.shape[0])
    for t in bases:
        coefs[t] = tiled[:, t * LANES : (t + 1) * LANES]
    coef = jnp.concatenate(
        [
            jnp.concatenate([coefs[t, pl.ds(c, boxes, stride=2), :] for t in bases], 1)
            for c in range(2)
        ],
        0,
    ).astype(BF16)

    rad_copy.wait()
    rad[...] = raw[...].reshape(rad.shape)
    work[...] = lax.dot_general(
        rad[...], coef, (((1,), (1,)), ((), ())), preferred_element_type=F32
    )
    by_real = work[pl.ds(0, q0, stride=2), :]
    by_imag = work[pl.ds(1, q0, stride=2), :]
    leaf_t = jnp.concatenate(
        [by_real[:, :boxes] - by_imag[:, boxes:], by_imag[:, :boxes] + by_real[:, boxes:]], 1
    )
    leaf = leaf_t.T.astype(BF16)

    def up_chunk(i):
        cols = pl.ds(i * chunk, chunk)
        co = cosv[:, cols]
        si = sinv[:, cols]
        int_copy(i).wait()
        up = jnp.dot(leaf, itp[:, cols], preferred_element_type=F32)
        for p in range(2):
            ur = up[8 * p : 8 * p + 8]
            ui = up[boxes + 8 * p : boxes + 8 * p + 8]
            outg[pl.ds(p, 1), cols] = jnp.sum(co * ur - si * ui, 0, keepdims=True)
            outg[pl.ds(2 + p, 1), cols] = jnp.sum(co * ui + si * ur, 0, keepdims=True)

    early = parts * 3 // 4
    for i in range(early):
        up_chunk(i)

    pl.semaphore_wait(barrier, n_wide - 1 + 4)

    def list_copy(w, there):
        return pltpu.make_async_remote_copy(
            src_ref=list_send, dst_ref=list_got.at[there], send_sem=list_ss, recv_sem=list_rs,
            device_id=(w, me_n), device_id_type=MESH)

    for w, there in peers[:-1]:
        list_copy(w, there).start()
    list_got[n_wide - 1] = list_send[...]

    for i in range(early, parts):
        up_chunk(i)

    for w in range(n_wide):
        tile, off = divmod(w * dirs, LANES)
        piece = outg[:, pl.ds(tile * LANES, LANES)]
        if off:
            piece = pltpu.roll(piece, LANES - off, 1)
            if off + dirs > LANES:
                more = pltpu.roll(outg[:, pl.ds((tile + 1) * LANES, LANES)], LANES - off, 1)
                at = lax.broadcasted_iota(jnp.int32, piece.shape, 1)
                piece = jnp.where(at < LANES - off, piece, more)
        x_send[w, :, pl.ds(0, LANES)] = piece[0:2]
        x_send[w, :, pl.ds(LANES, LANES)] = piece[2:4]

    def slice_copy(src_all, at, dst_all, there, w, send_sem, recv_sem):
        return pltpu.make_async_remote_copy(
            src_ref=src_all.at[at], dst_ref=dst_all.at[there], send_sem=send_sem,
            recv_sem=recv_sem, device_id=(w, me_n), device_id_type=MESH)

    def all_of(src_all, dst_all, send_sem, recv_sem, first=0, count=n_wide - 1):
        some = pl.ds(first, count)
        return pltpu.make_async_remote_copy(
            src_ref=src_all.at[some], dst_ref=dst_all.at[some], send_sem=send_sem,
            recv_sem=recv_sem, device_id=(peers[0][0], me_n), device_id_type=MESH)

    for w, there in peers[:-1]:
        slice_copy(x_send, w, x_got, there, w, x_ss, x_rs.at[there // per_chunk]).start()
    x_got[n_wide - 1] = x_send[me_w]

    lane_at = lax.broadcasted_iota(jnp.int32, (GROUP * per_share, LANES), 1)
    rows_all = n_narrow * n_rows
    spot = lax.broadcasted_iota(jnp.int32, (8, rows_all), 1)
    per_part = 2 * per_chunk
    place_of = (spot // (n_narrow * per_part)) * per_chunk + spot % per_part // 2
    holds = jnp.zeros((8, rows_all), jnp.int32)
    for i, (w, _) in enumerate(peers):
        holds = jnp.where(place_of == i, w, holds)
    holds = spot // per_part % n_narrow * n_rows + holds * 2 + spot % 2
    row_at = [
        jnp.broadcast_to(holds[0:1, t : t + LANES], (GROUP * per_share, LANES))
        for t in range(0, rows_all, LANES)
    ]

    all_of(list_got, list_got, list_ss, list_rs).wait_recv()
    for h in range(SHARES):
        mine = slice(h * n_wide // SHARES, (h + 1) * n_wide // SHARES)
        for t in range(STEPS):
            lists[h * STEPS + t] = list_got[mine, :, t * LANES : (t + 1) * LANES].reshape(
                per_share, LANES
            )

    def entries(g):
        here = lists[g]
        columns = [here[:, u : u + 1] for u in range(GROUP)]
        return jnp.concatenate([jnp.broadcast_to(c, (per_share, LANES)) for c in columns], 0)

    def one_hot(index, lanes):
        tiles = [jnp.where(index == at, 1.0, 0.0).astype(BF16) for at in lanes]
        return jnp.concatenate(tiles, 1)

    operators_at = [lane_at + t for t in range(0, tab.shape[0], LANES)]

    def pick_operators(g, c):
        onehot = one_hot(entries(g) & 511, operators_at)
        picks[g] = jnp.dot(onehot, tab[...], preferred_element_type=F32).astype(BF16)
        return c

    def pick(first, last):
        lax.fori_loop(first, last, pick_operators, 0)

    def block_copy(c, block, to):
        return pltpu.make_async_remote_copy(
            src_ref=x_all.at[c, block], dst_ref=x_all.at[c, block], send_sem=n_ss,
            recv_sem=n_rs.at[c * n_narrow + block], device_id=(me_w, to), device_id_type=MESH)

    def gather_slices(c):
        first = c * per_chunk
        count = per_chunk if c == 0 else per_chunk - 1
        all_of(x_got, x_got, x_ss, x_rs.at[c], first, count).wait_recv()
        x_all[c, me_n] = x_got[first : first + per_chunk].reshape(per_part, 2 * LANES)
        for to in (n_up, n_dn, n_par):
            block_copy(c, me_n, to).start()

    def pass_on(c):
        block_copy(c, n_dn, n_up).wait_recv()
        for to in (n_up, n_cross, n_par):
            block_copy(c, n_dn, to).start()
        block_copy(c, n_up, n_up).wait_recv()
        block_copy(c, n_up, n_par).start()

    pick(0, 1)
    gather_slices(1)
    pick(1, 2)
    gather_slices(0)
    pick(2, 3)
    pass_on(1)
    pick(3, 5)
    pass_on(0)
    pick(5, SHARES * STEPS)
    for c in range(CHUNKS):
        for n in (n_far, n_par, n_par + n_up - me_n, n_par + n_dn - me_n, n_par + n_far - me_n):
            block_copy(c, n, n_up).wait_recv()
    pat = x_all[...].astype(BF16).reshape(rows_all, 2 * LANES)

    def translate(g, c):
        onehot = one_hot(lax.shift_right_logical(entries(g), 9), row_at)
        px = jnp.dot(onehot, pat, preferred_element_type=F32)
        pt = picks[g].astype(F32)
        xr, xi = px[:, :LANES], px[:, LANES:]
        tr, ti = pt[:, :LANES], pt[:, LANES:]
        real = (tr * xr - ti * xi).reshape(GROUP, per_share, LANES).sum(0)
        imag = (tr * xi + ti * xr).reshape(GROUP, per_share, LANES).sum(0)
        return c[0] + real, c[1] + imag

    for h in range(SHARES):
        zero = jnp.zeros((per_share, LANES), F32)
        real, imag = lax.fori_loop(h * STEPS, (h + 1) * STEPS, translate, (zero, zero))
        mine = slice(h * n_wide // SHARES, (h + 1) * n_wide // SHARES)
        r_send[mine, :, pl.ds(0, LANES)] = real.reshape(-1, 2, LANES)
        r_send[mine, :, pl.ds(LANES, LANES)] = imag.reshape(-1, 2, LANES)
        for i in range(mine.start, min(mine.stop, n_wide - 1)):
            slice_copy(r_send, i, r_got, me_w, peers[i][0], r_ss, r_rs).start()
    r_got[me_w] = r_send[n_wide - 1]
    all_of(r_got, r_got, r_ss, r_rs).wait_recv()

    tiles = [None] * (q1 // LANES)
    at = lax.broadcasted_iota(jnp.int32, (4, LANES), 1)
    for w in range(n_wide):
        tile, off = divmod(w * dirs, LANES)
        piece = jnp.concatenate(
            [r_got[w, :, pl.ds(0, LANES)], r_got[w, :, pl.ds(LANES, LANES)]], 0
        )
        if off:
            piece = pltpu.roll(piece, off, 1)
        if tiles[tile] is None:
            tiles[tile] = piece
        else:
            tiles[tile] = jnp.where(at < off, tiles[tile], piece)
        if off + dirs > LANES:
            tiles[tile + 1] = piece
    for i, tile in enumerate(tiles):
        inc[:, pl.ds(i * LANES, LANES)] = tile

    for i in range(parts):
        cols = pl.ds(i * chunk, chunk)
        co = cosv[:, cols]
        si = sinv[:, cols]
        real, imag = [], []
        for p in range(2):
            ir = inc[pl.ds(p, 1), cols]
            ii = inc[pl.ds(2 + p, 1), cols]
            real.append(co * ir + si * ii)
            imag.append(co * ii - si * ir)
        down[:, cols] = jnp.concatenate(real + imag, 0).astype(BF16)
    recv_acc[...] = lax.dot_general(
        itp[...], down[...], (((1,), (1,)), ((), ())), preferred_element_type=F32
    )

    got_t = recv_acc[...]
    work[pl.ds(0, q0, stride=2), :] = got_t
    work[pl.ds(1, q0, stride=2), :] = jnp.concatenate([got_t[:, boxes:], -got_t[:, :boxes]], 1)
    out_ref[...] = jnp.dot(work[...].T.astype(BF16), rad[...], preferred_element_type=F32)
    all_of(list_got, list_got, list_ss, list_rs).wait_send()
    all_of(x_send, x_got, x_ss, x_rs.at[0]).wait_send()
    all_of(r_send, r_got, r_ss, r_rs).wait_send()
    for c in range(CHUNKS):
        pltpu.make_async_remote_copy(
            src_ref=x_all.at[c, pl.ds(0, n_narrow - 1)],
            dst_ref=x_all.at[c, pl.ds(0, n_narrow - 1)],
            send_sem=n_ss, recv_sem=n_rs.at[0], device_id=(me_w, n_up), device_id_type=MESH,
        ).wait_send()


def solution(mesh):
    n_wide, n_narrow = mesh.shape["wide"], mesh.shape["narrow"]
    n_z = 8
    both = ("wide", "narrow")

    def on_device(coef, rad, interp, angles, table, sources, operators, counts):
        boxes, _, n_bases = coef.shape
        q0, q1 = interp.shape
        n_ops = table.shape[0]
        n_list = sources.shape[1]
        chunk = 256
        parts = q1 // chunk
        rows = 2 * n_wide
        rad_raw = jnp.transpose(rad, (2, 0, 1))
        table_t = jnp.transpose(table, (1, 2, 0))
        n_tab = -(-n_ops // LANES) * LANES
        assert n_list <= GROUP * STEPS
        vmem = pl.BlockSpec(memory_space=pltpu.VMEM)
        anyw = pl.BlockSpec(memory_space=pl.ANY)
        dma = pltpu.SemaphoreType.DMA
        slots = (n_wide, 2, 2 * LANES)
        result = pl.pallas_call(
            functools.partial(kernel, (n_wide, n_narrow, n_z, chunk)),
            out_shape=jax.ShapeDtypeStruct((2 * boxes, n_bases), F32),
            in_specs=[anyw] * 8,
            out_specs=vmem,
            scratch_shapes=[
                pltpu.SMEM(counts.shape, jnp.int32),
                pltpu.VMEM(coef.shape, BF16),
                pltpu.VMEM(angles.shape, F32),
                pltpu.VMEM(table_t.shape, F32),
                pltpu.VMEM(sources.shape, jnp.int32),
                pltpu.VMEM(operators.shape, jnp.int32),
                pltpu.VMEM((q0, 2, n_bases), BF16),
                pltpu.VMEM((2 * q0, n_bases), BF16),
                pltpu.VMEM((q0, q1), BF16),
                pltpu.VMEM((8, q1), F32),
                pltpu.VMEM((8, q1), F32),
                pltpu.VMEM((2 * q0, 2 * boxes), F32),
                pltpu.VMEM((n_bases // LANES, 2 * boxes, LANES), F32),
                pltpu.VMEM((4, q1), F32),
                pltpu.VMEM((2, 2 * LANES), jnp.int32),
                pltpu.VMEM(slots, jnp.int32),
                pltpu.VMEM((SHARES * STEPS, rows // SHARES, LANES), jnp.int32),
                pltpu.VMEM(slots, F32),
                pltpu.VMEM(slots, F32),
                pltpu.VMEM((CHUNKS, n_narrow, rows // CHUNKS, 2 * LANES), F32),
                pltpu.VMEM((n_tab, 2 * LANES), BF16),
                pltpu.VMEM((SHARES * STEPS, GROUP * rows // SHARES, 2 * LANES), BF16),
                pltpu.VMEM((2 * boxes, q1), BF16),
                pltpu.VMEM(slots, F32),
                pltpu.VMEM(slots, F32),
                pltpu.VMEM((4, q1), F32),
                pltpu.VMEM((q0, 2 * boxes), F32),
                dma((parts + 7,)),
                dma, dma, dma, dma((CHUNKS,)), dma, dma((CHUNKS * n_narrow,)), dma, dma,
            ],
            compiler_params=pltpu.CompilerParams(
                collective_id=0, has_side_effects=True, vmem_limit_bytes=60 * 1024 * 1024
            ),
            name="fmm_step",
        )(counts, coef, rad_raw, interp, angles, table_t, sources, operators)
        return jnp.transpose(result.reshape(2, boxes, n_bases), (1, 0, 2))

    return jax.shard_map(
        on_device,
        mesh=mesh,
        in_specs=(
            P(both, None, None), P(), P(), P(), P(None, None, "wide"),
            P(both, None), P(both, None), P(both),
        ),
        out_specs=P(both, None, None),
        check_vma=False,
    )
```

```python
import functools

import jax
import jax.numpy as jnp
from jax import lax
from jax.experimental import pallas as pl
from jax.experimental.pallas import tpu as pltpu
from jax.sharding import PartitionSpec as P

MESH = pl.DeviceIdType.MESH
BF16 = jnp.bfloat16
F32 = jnp.float32
LANES = 128
GROUP = 96
STEPS = 2
SHARES = 4
CHUNKS = 2
ROWS = 112
FIELDS = 3
NO_OPERATOR = 511


def offsets_along(n_x, n_z):
    def hops(o):
        return min(o[0], n_x - o[0]) + min(o[1], n_z - o[1])

    return sorted(((a, b) for a in range(n_x) for b in range(n_z)), key=lambda o: (-hops(o), o))


def kernel(
    dims,
    counts_hbm, coef_hbm, rad_hbm, int_hbm, ang_hbm, tab_hbm, src_hbm, opr_hbm,
    out_ref,
    counts_ref, coef_ref, ang_ref, tab_ref, src_ref, opr_ref,
    raw, rad, itp, cosv, sinv, work, planes, coefs, outg, list_send, list_got, lists, x_send, x_got, x_all,
    tab, picks, down, r_send, r_got, inc,
    mem_sem, list_ss, list_rs, x_ss, x_rs, n_ss, n_rs, r_ss, r_rs,
):
    n_wide, n_narrow, n_z, chunk = dims
    n_x = n_wide // n_z
    me_w = lax.axis_index("wide")
    me_n = lax.axis_index("narrow")
    me_x, me_z = me_w // n_z, me_w % n_z
    q0, q1 = int_hbm.shape
    parts = q1 // chunk
    dirs = q1 // n_wide
    n_list = src_ref.shape[1]
    n_rows = 2 * n_wide
    per_share = n_rows // SHARES
    per_chunk = n_wide // CHUNKS
    boxes = coef_ref.shape[0]

    small = [
        pltpu.make_async_copy(a, b, mem_sem.at[parts + i])
        for i, (a, b) in enumerate([
            (coef_hbm, coef_ref), (src_hbm, src_ref), (opr_hbm, opr_ref),
            (counts_hbm, counts_ref), (ang_hbm, ang_ref), (tab_hbm, tab_ref),
        ])
    ]
    small[0].start()
    blocks = [(q, min(q + ROWS, q0)) for q in range(0, q0, ROWS)]
    rad_copies = [
        pltpu.make_async_copy(rad_hbm.at[a:b], raw.at[a:b], mem_sem.at[parts + 6 + i])
        for i, (a, b) in enumerate(blocks)
    ]
    for copy in rad_copies + small[1:5]:
        copy.start()

    def int_copy(i):
        cols = pl.ds(i * chunk, chunk)
        return pltpu.make_async_copy(int_hbm.at[:, cols], itp.at[:, cols], mem_sem.at[i])

    barrier = pltpu.get_barrier_semaphore()
    offsets = offsets_along(n_x, n_z)
    place = {o: i for i, o in enumerate(offsets)}
    peers = []
    for dx, dz in offsets:
        w = lax.rem(me_x + dx, n_x) * n_z + lax.rem(me_z + dz, n_z)
        peers.append((w, place[(-dx) % n_x, (-dz) % n_z]))
    for w, _ in peers[:-1]:
        pl.semaphore_signal(barrier, 1, device_id=(w, me_n), device_id_type=MESH)
    me_y, me_c = me_n // 2, me_n % 2
    n_y = n_narrow // 2
    ahead = 1 - 2 * me_c
    n_up = lax.rem(me_y + ahead + n_y, n_y) * 2 + me_c
    n_dn = lax.rem(me_y - ahead + n_y, n_y) * 2 + me_c
    n_far = lax.rem(me_y + 2, n_y) * 2 + me_c
    n_par = me_y * 2 + 1 - me_c
    n_cross = n_up + ahead
    for n in (n_up, n_dn, n_par, n_cross):
        pl.semaphore_signal(barrier, 1, device_id=(me_w, n), device_id_type=MESH)

    for i in range(parts):
        int_copy(i).start()
    small[5].start()

    small[0].wait()
    tiled = coef_ref[...].astype(F32).reshape(2 * boxes, -1)
    bases = range(coefs.shape[0])
    for t in bases:
        coefs[t] = tiled[:, t * LANES : (t + 1) * LANES]
    real, imag = [
        jnp.concatenate([coefs[t, pl.ds(c, boxes, stride=2), :] for t in bases], 1)
        for c in range(2)
    ]
    coef = jnp.concatenate(
        [jnp.concatenate([real, -imag], 1), jnp.concatenate([imag, real], 1)], 0
    ).astype(BF16)

    n_bases = rad_hbm.shape[2]
    for copy, (a, b) in zip(rad_copies, blocks):
        copy.wait()
        rows = pl.ds(2 * a, 2 * (b - a))
        rad[rows, :] = raw[a:b].reshape(2 * (b - a), n_bases)
        for t in bases:
            work[t, rows, :] = rad[rows, pl.ds(t * LANES, LANES)].astype(F32)
            for c in range(2):
                planes[pl.ds(a, b - a), pl.ds(c * n_bases + t * LANES, LANES)] = work[
                    t, pl.ds(2 * a + c, b - a, stride=2), :
                ].astype(BF16)
    leaf = lax.dot_general(
        coef, planes[...], (((1,), (1,)), ((), ())), preferred_element_type=F32
    ).astype(BF16)

    def up_chunk(i):
        cols = pl.ds(i * chunk, chunk)
        ang = ang_ref[:, cols]
        co = jnp.cos(ang)
        si = jnp.sin(ang)
        cosv[:, cols] = co
        sinv[:, cols] = si
        up = jnp.dot(leaf, itp[:, cols], preferred_element_type=F32)
        for p in range(2):
            ur = up[8 * p : 8 * p + 8]
            ui = up[boxes + 8 * p : boxes + 8 * p + 8]
            outg[pl.ds(p, 1), cols] = jnp.sum(co * ur - si * ui, 0, keepdims=True)
            outg[pl.ds(2 + p, 1), cols] = jnp.sum(co * ui + si * ur, 0, keepdims=True)

    small[4].wait()
    groups = [(0, 4), (4, 8), (8, 11), (11, parts)]

    def up_group(first, last):
        for i in range(first, last):
            int_copy(i).wait()
        for i in range(first, last):
            up_chunk(i)

    for g in groups[:-1]:
        up_group(*g)

    for copy in small[1:4]:
        copy.wait()
    src = src_ref[...]
    opr = opr_ref[...]
    half = lax.shift_right_logical(src, 1)
    row = (half % n_narrow) * n_rows + (half // n_narrow) * 2 + (src & 1)
    lane = lax.broadcasted_iota(jnp.int32, src.shape, 1)
    which = lax.broadcasted_iota(jnp.int32, src.shape, 0)
    limit = jnp.where(which == 0, counts_ref[0], counts_ref[1])
    wanted = jnp.where(lane < limit, opr, NO_OPERATOR)
    n_words = n_list // FIELDS
    at = lax.broadcasted_iota(jnp.int32, (1, LANES), 1)
    for kind, value in enumerate((wanted, row)):
        value = jnp.concatenate(
            [value, jnp.full((2, 2 * LANES - n_list), NO_OPERATOR, jnp.int32)], 1
        )
        word = jnp.zeros((2, LANES), jnp.int32)
        for k in range(FIELDS):
            word = word + (pltpu.roll(value, (2 * LANES - k * n_words) % (2 * LANES), 1)[:, :LANES] << (9 * k))
        list_send[pl.ds(kind, 1), :] = jnp.where(
            at < LANES // 2, word[0:1], pltpu.roll(word[1:2], LANES // 2, 1)
        )

    up_group(*groups[-1])

    for w in range(n_wide):
        tile, off = divmod(w * dirs, LANES)
        piece = outg[:, pl.ds(tile * LANES, LANES)]
        if off:
            piece = pltpu.roll(piece, LANES - off, 1)
            if off + dirs > LANES:
                more = pltpu.roll(outg[:, pl.ds((tile + 1) * LANES, LANES)], LANES - off, 1)
                at = lax.broadcasted_iota(jnp.int32, piece.shape, 1)
                piece = jnp.where(at < LANES - off, piece, more)
        x_send[w, :, pl.ds(0, LANES)] = piece[0:2]
        x_send[w, :, pl.ds(LANES, LANES)] = piece[2:4]

    def slice_copy(src_all, at, dst_all, there, w, send_sem, recv_sem):
        return pltpu.make_async_remote_copy(
            src_ref=src_all.at[at], dst_ref=dst_all.at[there], send_sem=send_sem,
            recv_sem=recv_sem, device_id=(w, me_n), device_id_type=MESH)

    def all_of(src_all, dst_all, send_sem, recv_sem, first=0, count=n_wide - 1):
        some = pl.ds(first, count)
        return pltpu.make_async_remote_copy(
            src_ref=src_all.at[some], dst_ref=dst_all.at[some], send_sem=send_sem,
            recv_sem=recv_sem, device_id=(peers[0][0], me_n), device_id_type=MESH)

    pl.semaphore_wait(barrier, n_wide - 1 + 4)
    for w, there in peers[:-1]:
        slice_copy(x_send, w, x_got, there, w, x_ss, x_rs.at[there // per_chunk]).start()
    x_got[n_wide - 1] = x_send[me_w]

    def list_copy(w, there):
        return pltpu.make_async_remote_copy(
            src_ref=list_send, dst_ref=list_got.at[there], send_sem=list_ss, recv_sem=list_rs,
            device_id=(w, me_n), device_id_type=MESH)

    for w, there in peers[:-1]:
        list_copy(w, there).start()
    list_got[n_wide - 1] = list_send[...]


    small[5].wait()
    n_ops = tab_ref.shape[2]
    for c in range(2):
        t = tab_ref[c]
        t = jnp.concatenate([t, jnp.zeros((LANES - dirs, n_ops), F32)], 0)
        t = jnp.concatenate([t, jnp.zeros((LANES, tab.shape[0] - n_ops), F32)], 1)
        tab[:, pl.ds(c * LANES, LANES)] = t.T.astype(BF16)

    lane_at = lax.broadcasted_iota(jnp.int32, (GROUP * per_share, LANES), 1)
    rows_all = n_narrow * n_rows
    spot = lax.broadcasted_iota(jnp.int32, (8, rows_all), 1)
    per_part = 2 * per_chunk
    place_of = (spot // (n_narrow * per_part)) * per_chunk + spot % per_part // 2
    holds = jnp.zeros((8, rows_all), jnp.int32)
    for i, (w, _) in enumerate(peers):
        holds = jnp.where(place_of == i, w, holds)
    holds = spot // per_part % n_narrow * n_rows + holds * 2 + spot % 2
    row_at = [
        jnp.broadcast_to(holds[0:1, t : t + LANES], (GROUP * per_share, LANES))
        for t in range(0, rows_all, LANES)
    ]

    def entries(g, kind):
        here = lists[kind, g]
        columns = [here[:, u : u + 1] for u in range(GROUP)]
        return jnp.concatenate([jnp.broadcast_to(c, (per_share, LANES)) for c in columns], 0)

    def one_hot(index, lanes):
        tiles = [jnp.where(index == at, 1.0, 0.0).astype(BF16) for at in lanes]
        return jnp.concatenate(tiles, 1)

    operators_at = [lane_at + t for t in range(0, tab.shape[0], LANES)]

    def pick_operators(g, c):
        onehot = one_hot(entries(g, 0), operators_at)
        picks[g] = jnp.dot(onehot, tab[...], preferred_element_type=F32)
        return c

    def pick(first, last):
        lax.fori_loop(first, last, pick_operators, 0)

    def block_copy(c, block, to):
        return pltpu.make_async_remote_copy(
            src_ref=x_all.at[c, block], dst_ref=x_all.at[c, block], send_sem=n_ss,
            recv_sem=n_rs.at[c * n_narrow + block], device_id=(me_w, to), device_id_type=MESH)

    def gather_slices(c):
        first = c * per_chunk
        count = per_chunk if c == 0 else per_chunk - 1
        all_of(x_got, x_got, x_ss, x_rs.at[c], first, count).wait_recv()
        x_all[c, me_n] = x_got[first : first + per_chunk].reshape(per_part, 2 * LANES)
        for to in (n_up, n_dn, n_par):
            block_copy(c, me_n, to).start()

    def pass_on(c):
        block_copy(c, n_dn, n_up).wait_recv()
        for to in (n_up, n_cross, n_par):
            block_copy(c, n_dn, to).start()
        block_copy(c, n_up, n_up).wait_recv()
        block_copy(c, n_up, n_par).start()

    gather_slices(1)
    gather_slices(0)
    all_of(list_got, list_got, list_ss, list_rs).wait_recv()
    first = GROUP - n_words
    lane = lax.broadcasted_iota(jnp.int32, (per_share, LANES), 1)
    for h in range(SHARES):
        mine = slice(h * n_wide // SHARES, (h + 1) * n_wide // SHARES)
        for kind in range(2):
            words = list_got[mine, kind, :]
            words = jnp.concatenate([words, pltpu.roll(words, LANES // 2, 1)], 0)
            field = [lax.shift_right_logical(words, 9 * k) & 511 for k in range(FIELDS)]
            early = jnp.where(lane < n_words, field[0], pltpu.roll(field[1], n_words, 1))
            late = jnp.where(lane < n_words, field[2], pltpu.roll(field[1], n_words - first, 1))
            lists[kind, h * STEPS] = early
            lists[kind, h * STEPS + 1] = jnp.where(lane < n_list - GROUP, late, NO_OPERATOR)
    pass_on(1)
    pick(0, 2)
    pass_on(0)
    pick(2, SHARES * STEPS)
    for c in range(CHUNKS):
        for n in (n_far, n_par, n_par + n_up - me_n, n_par + n_dn - me_n, n_par + n_far - me_n):
            block_copy(c, n, n_up).wait_recv()
    pat = x_all[...].astype(BF16).reshape(rows_all, 2 * LANES)

    def translate(g, c):
        onehot = one_hot(entries(g, 1), row_at)
        px = jnp.dot(onehot, pat, preferred_element_type=F32)
        pt = picks[g]
        xr, xi = px[:, :LANES], px[:, LANES:]
        tr, ti = pt[:, :LANES], pt[:, LANES:]
        real = (tr * xr - ti * xi).reshape(GROUP, per_share, LANES).sum(0)
        imag = (tr * xi + ti * xr).reshape(GROUP, per_share, LANES).sum(0)
        return c[0] + real, c[1] + imag

    for h in range(SHARES):
        zero = jnp.zeros((per_share, LANES), F32)
        real, imag = lax.fori_loop(h * STEPS, (h + 1) * STEPS, translate, (zero, zero))
        mine = slice(h * n_wide // SHARES, (h + 1) * n_wide // SHARES)
        for j in range(2):
            rows = slice(j * per_share // 2, (j + 1) * per_share // 2)
            r_send[mine, j, pl.ds(0, LANES)] = real[rows]
            r_send[mine, j, pl.ds(LANES, LANES)] = imag[rows]
        for i in range(mine.start, min(mine.stop, n_wide - 1)):
            slice_copy(r_send, i, r_got, me_w, peers[i][0], r_ss, r_rs).start()
    r_got[me_w] = r_send[n_wide - 1]
    all_of(r_got, r_got, r_ss, r_rs).wait_recv()

    tiles = [None] * (q1 // LANES)
    at = lax.broadcasted_iota(jnp.int32, (4, LANES), 1)
    for w in range(n_wide):
        tile, off = divmod(w * dirs, LANES)
        piece = jnp.concatenate(
            [r_got[w, :, pl.ds(0, LANES)], r_got[w, :, pl.ds(LANES, LANES)]], 0
        )
        if off:
            piece = pltpu.roll(piece, off, 1)
        if tiles[tile] is None:
            tiles[tile] = piece
        else:
            tiles[tile] = jnp.where(at < off, tiles[tile], piece)
        if off + dirs > LANES:
            tiles[tile + 1] = piece
    for i, tile in enumerate(tiles):
        inc[:, pl.ds(i * LANES, LANES)] = tile

    for i in range(parts):
        cols = pl.ds(i * chunk, chunk)
        co = cosv[:, cols]
        si = sinv[:, cols]
        real, imag = [], []
        for p in range(2):
            ir = inc[pl.ds(p, 1), cols]
            ii = inc[pl.ds(2 + p, 1), cols]
            real.append(co * ir + si * ii)
            imag.append(co * ii - si * ir)
        down[:, cols] = jnp.concatenate(real + imag, 0).astype(BF16)
    received = lax.dot_general(
        down[...], itp[...], (((1,), (1,)), ((), ())), preferred_element_type=F32
    ).astype(BF16)

    both = jnp.dot(received, planes[...], preferred_element_type=F32)
    by_real, by_imag = both[:, :n_bases], both[:, n_bases:]
    out_ref[pl.ds(0, boxes), :] = by_real[:boxes] + by_imag[boxes:]
    out_ref[pl.ds(boxes, boxes), :] = by_real[boxes:] - by_imag[:boxes]

    all_of(list_got, list_got, list_ss, list_rs).wait_send()
    all_of(x_send, x_got, x_ss, x_rs.at[0]).wait_send()
    all_of(r_send, r_got, r_ss, r_rs).wait_send()
    for c in range(CHUNKS):
        pltpu.make_async_remote_copy(
            src_ref=x_all.at[c, pl.ds(0, n_narrow - 1)],
            dst_ref=x_all.at[c, pl.ds(0, n_narrow - 1)],
            send_sem=n_ss, recv_sem=n_rs.at[0], device_id=(me_w, n_up), device_id_type=MESH,
        ).wait_send()


def solution(mesh):
    n_wide, n_narrow = mesh.shape["wide"], mesh.shape["narrow"]
    n_z = 8
    both = ("wide", "narrow")

    def on_device(coef, rad, interp, angles, table, sources, operators, counts):
        boxes, _, n_bases = coef.shape
        q0, q1 = interp.shape
        n_ops = table.shape[0]
        n_list = sources.shape[1]
        chunk = 256
        parts = q1 // chunk
        rows = 2 * n_wide
        rad_raw = jnp.transpose(rad, (2, 0, 1))
        table_t = jnp.transpose(table, (1, 2, 0))
        n_tab = -(-n_ops // LANES) * LANES
        assert n_list % FIELDS == 0 and n_list <= GROUP * STEPS
        assert n_list // FIELDS <= LANES // 2
        vmem = pl.BlockSpec(memory_space=pltpu.VMEM)
        anyw = pl.BlockSpec(memory_space=pl.ANY)
        dma = pltpu.SemaphoreType.DMA
        slots = (n_wide, 2, 2 * LANES)
        result = pl.pallas_call(
            functools.partial(kernel, (n_wide, n_narrow, n_z, chunk)),
            out_shape=jax.ShapeDtypeStruct((2 * boxes, n_bases), F32),
            in_specs=[anyw] * 8,
            out_specs=vmem,
            scratch_shapes=[
                pltpu.SMEM(counts.shape, jnp.int32),
                pltpu.VMEM(coef.shape, BF16),
                pltpu.VMEM(angles.shape, F32),
                pltpu.VMEM(table_t.shape, F32),
                pltpu.VMEM(sources.shape, jnp.int32),
                pltpu.VMEM(operators.shape, jnp.int32),
                pltpu.VMEM((q0, 2, n_bases), BF16),
                pltpu.VMEM((2 * q0, n_bases), BF16),
                pltpu.VMEM((q0, q1), BF16),
                pltpu.VMEM((8, q1), F32),
                pltpu.VMEM((8, q1), F32),
                pltpu.VMEM((n_bases // LANES, 2 * q0, LANES), F32),
                pltpu.VMEM((q0, 2 * n_bases), BF16),
                pltpu.VMEM((n_bases // LANES, 2 * boxes, LANES), F32),
                pltpu.VMEM((4, q1), F32),
                pltpu.VMEM((2, LANES), jnp.int32),
                pltpu.VMEM((n_wide, 2, LANES), jnp.int32),
                pltpu.VMEM((2, SHARES * STEPS, rows // SHARES, LANES), jnp.int32),
                pltpu.VMEM(slots, F32),
                pltpu.VMEM(slots, F32),
                pltpu.VMEM((CHUNKS, n_narrow, rows // CHUNKS, 2 * LANES), F32),
                pltpu.VMEM((n_tab, 2 * LANES), BF16),
                pltpu.VMEM((SHARES * STEPS, GROUP * rows // SHARES, 2 * LANES), F32),
                pltpu.VMEM((2 * boxes, q1), BF16),
                pltpu.VMEM(slots, F32),
                pltpu.VMEM(slots, F32),
                pltpu.VMEM((4, q1), F32),
                dma((parts + 6 + -(-q0 // ROWS),)),
                dma, dma, dma, dma((CHUNKS,)), dma, dma((CHUNKS * n_narrow,)), dma, dma,
            ],
            compiler_params=pltpu.CompilerParams(
                collective_id=0, has_side_effects=True, vmem_limit_bytes=60 * 1024 * 1024
            ),
            name="fmm_step",
        )(counts, coef, rad_raw, interp, angles, table_t, sources, operators)
        return jnp.transpose(result.reshape(2, boxes, n_bases), (1, 0, 2))

    return jax.shard_map(
        on_device,
        mesh=mesh,
        in_specs=(
            P(both, None, None), P(), P(), P(), P(None, None, "wide"),
            P(both, None), P(both, None), P(both),
        ),
        out_specs=P(both, None, None),
        check_vma=False,
    )
```

```python
import functools

import jax
import jax.numpy as jnp
from jax import lax
from jax.experimental import pallas as pl
from jax.experimental.pallas import tpu as pltpu
from jax.sharding import PartitionSpec as P

MESH = pl.DeviceIdType.MESH
BF16 = jnp.bfloat16
F32 = jnp.float32
LANES = 128
GROUP = 96
STEPS = 2
SHARES = 4
CHUNKS = 2
ROWS = 112
FIELDS = 3
NO_OPERATOR = 511


def offsets_along(n_x, n_z):
    def hops(o):
        return min(o[0], n_x - o[0]) + min(o[1], n_z - o[1])

    return sorted(((a, b) for a in range(n_x) for b in range(n_z)), key=lambda o: (-hops(o), o))


def kernel(
    dims,
    counts_hbm, coef_hbm, rad_hbm, int_hbm, ang_hbm, tab_hbm, src_hbm, opr_hbm,
    out_ref,
    counts_ref, coef_ref, ang_ref, tab_ref, src_ref, opr_ref,
    raw, rad, itp, cosv, sinv, work, planes, coefs, outg, list_send, list_got, lists, x_send, x_got, x_all,
    tab, picks, down, r_send, r_got, inc,
    mem_sem, list_ss, list_rs, x_ss, x_rs, n_ss, n_rs, r_ss, r_rs,
):
    n_wide, n_narrow, n_z, chunk = dims
    n_x = n_wide // n_z
    me_w = lax.axis_index("wide")
    me_n = lax.axis_index("narrow")
    me_x, me_z = me_w // n_z, me_w % n_z
    q0, q1 = int_hbm.shape
    parts = q1 // chunk
    dirs = q1 // n_wide
    n_list = src_ref.shape[1]
    n_rows = 2 * n_wide
    per_share = n_rows // SHARES
    per_chunk = n_wide // CHUNKS
    boxes = coef_ref.shape[0]

    small = [
        pltpu.make_async_copy(a, b, mem_sem.at[parts + i])
        for i, (a, b) in enumerate([
            (coef_hbm, coef_ref), (src_hbm, src_ref), (opr_hbm, opr_ref),
            (counts_hbm, counts_ref), (ang_hbm, ang_ref), (tab_hbm, tab_ref),
        ])
    ]
    small[0].start()
    blocks = [(q, min(q + ROWS, q0)) for q in range(0, q0, ROWS)]
    rad_copies = [
        pltpu.make_async_copy(rad_hbm.at[a:b], raw.at[a:b], mem_sem.at[parts + 6 + i])
        for i, (a, b) in enumerate(blocks)
    ]
    for copy in rad_copies + small[1:5]:
        copy.start()

    def int_copy(i):
        cols = pl.ds(i * chunk, chunk)
        return pltpu.make_async_copy(int_hbm.at[:, cols], itp.at[:, cols], mem_sem.at[i])

    barrier = pltpu.get_barrier_semaphore()
    offsets = offsets_along(n_x, n_z)
    place = {o: i for i, o in enumerate(offsets)}
    peers = []
    for dx, dz in offsets:
        w = lax.rem(me_x + dx, n_x) * n_z + lax.rem(me_z + dz, n_z)
        peers.append((w, place[(-dx) % n_x, (-dz) % n_z]))
    for w, _ in peers[:-1]:
        pl.semaphore_signal(barrier, 1, device_id=(w, me_n), device_id_type=MESH)
    me_y, me_c = me_n // 2, me_n % 2
    n_y = n_narrow // 2
    ahead = 1 - 2 * me_c
    n_up = lax.rem(me_y + ahead + n_y, n_y) * 2 + me_c
    n_dn = lax.rem(me_y - ahead + n_y, n_y) * 2 + me_c
    n_far = lax.rem(me_y + 2, n_y) * 2 + me_c
    n_par = me_y * 2 + 1 - me_c
    n_cross = n_up + ahead
    for n in (n_up, n_dn, n_par, n_cross):
        pl.semaphore_signal(barrier, 1, device_id=(me_w, n), device_id_type=MESH)

    for i in range(parts):
        int_copy(i).start()
    small[5].start()

    small[0].wait()
    tiled = coef_ref[...].astype(F32).reshape(2 * boxes, -1)
    bases = range(coefs.shape[0])
    for t in bases:
        coefs[t] = tiled[:, t * LANES : (t + 1) * LANES]
    real, imag = [
        jnp.concatenate([coefs[t, pl.ds(c, boxes, stride=2), :] for t in bases], 1)
        for c in range(2)
    ]
    coef = jnp.concatenate(
        [jnp.concatenate([real, -imag], 1), jnp.concatenate([imag, real], 1)], 0
    ).astype(BF16)

    n_bases = rad_hbm.shape[2]
    for copy, (a, b) in zip(rad_copies, blocks):
        copy.wait()
        rows = pl.ds(2 * a, 2 * (b - a))
        rad[rows, :] = raw[a:b].reshape(2 * (b - a), n_bases)
        for t in bases:
            work[t, rows, :] = rad[rows, pl.ds(t * LANES, LANES)].astype(F32)
            for c in range(2):
                planes[pl.ds(a, b - a), pl.ds(c * n_bases + t * LANES, LANES)] = work[
                    t, pl.ds(2 * a + c, b - a, stride=2), :
                ].astype(BF16)
    leaf = lax.dot_general(
        coef, planes[...], (((1,), (1,)), ((), ())), preferred_element_type=F32
    ).astype(BF16)

    def up_chunk(i):
        cols = pl.ds(i * chunk, chunk)
        ang = ang_ref[:, cols]
        co = jnp.cos(ang)
        si = jnp.sin(ang)
        cosv[:, cols] = co
        sinv[:, cols] = si
        up = jnp.dot(leaf, itp[:, cols], preferred_element_type=F32)
        for p in range(2):
            ur = up[8 * p : 8 * p + 8]
            ui = up[boxes + 8 * p : boxes + 8 * p + 8]
            outg[pl.ds(p, 1), cols] = jnp.sum(co * ur - si * ui, 0, keepdims=True)
            outg[pl.ds(2 + p, 1), cols] = jnp.sum(co * ui + si * ur, 0, keepdims=True)

    small[4].wait()
    groups = [(0, 4), (4, 8), (8, 11), (11, parts)]

    def up_group(first, last):
        for i in range(first, last):
            int_copy(i).wait()
        for i in range(first, last):
            up_chunk(i)

    for g in groups[:-1]:
        up_group(*g)

    for copy in small[1:4]:
        copy.wait()
    src = src_ref[...]
    opr = opr_ref[...]
    half = lax.shift_right_logical(src, 1)
    row = (half % n_narrow) * n_rows + (half // n_narrow) * 2 + (src & 1)
    lane = lax.broadcasted_iota(jnp.int32, src.shape, 1)
    which = lax.broadcasted_iota(jnp.int32, src.shape, 0)
    limit = jnp.where(which == 0, counts_ref[0], counts_ref[1])
    wanted = jnp.where(lane < limit, opr, NO_OPERATOR)
    n_words = n_list // FIELDS
    at = lax.broadcasted_iota(jnp.int32, (1, LANES), 1)
    for kind, value in enumerate((wanted, row)):
        value = jnp.concatenate(
            [value, jnp.full((2, 2 * LANES - n_list), NO_OPERATOR, jnp.int32)], 1
        )
        word = jnp.zeros((2, LANES), jnp.int32)
        for k in range(FIELDS):
            word = word + (pltpu.roll(value, (2 * LANES - k * n_words) % (2 * LANES), 1)[:, :LANES] << (9 * k))
        list_send[pl.ds(kind, 1), :] = jnp.where(
            at < LANES // 2, word[0:1], pltpu.roll(word[1:2], LANES // 2, 1)
        )

    up_group(*groups[-1])

    for w in range(n_wide):
        tile, off = divmod(w * dirs, LANES)
        piece = outg[:, pl.ds(tile * LANES, LANES)]
        if off:
            piece = pltpu.roll(piece, LANES - off, 1)
            if off + dirs > LANES:
                more = pltpu.roll(outg[:, pl.ds((tile + 1) * LANES, LANES)], LANES - off, 1)
                at = lax.broadcasted_iota(jnp.int32, piece.shape, 1)
                piece = jnp.where(at < LANES - off, piece, more)
        x_send[w, :, pl.ds(0, LANES)] = piece[0:2]
        x_send[w, :, pl.ds(LANES, LANES)] = piece[2:4]

    def slice_copy(src_all, at, dst_all, there, w, send_sem, recv_sem):
        return pltpu.make_async_remote_copy(
            src_ref=src_all.at[at], dst_ref=dst_all.at[there], send_sem=send_sem,
            recv_sem=recv_sem, device_id=(w, me_n), device_id_type=MESH)

    def all_of(src_all, dst_all, send_sem, recv_sem, first=0, count=n_wide - 1):
        some = pl.ds(first, count)
        return pltpu.make_async_remote_copy(
            src_ref=src_all.at[some], dst_ref=dst_all.at[some], send_sem=send_sem,
            recv_sem=recv_sem, device_id=(peers[0][0], me_n), device_id_type=MESH)

    pl.semaphore_wait(barrier, n_wide - 1 + 4)
    for w, there in peers[:-1]:
        slice_copy(x_send, w, x_got, there, w, x_ss, x_rs.at[there // per_chunk]).start()
    x_got[n_wide - 1] = x_send[me_w]

    def list_copy(w, there):
        return pltpu.make_async_remote_copy(
            src_ref=list_send, dst_ref=list_got.at[there], send_sem=list_ss, recv_sem=list_rs,
            device_id=(w, me_n), device_id_type=MESH)

    for w, there in peers[:-1]:
        list_copy(w, there).start()
    list_got[n_wide - 1] = list_send[...]


    small[5].wait()
    n_ops = tab_ref.shape[2]
    for c in range(2):
        t = tab_ref[c]
        t = jnp.concatenate([t, jnp.zeros((LANES - dirs, n_ops), F32)], 0)
        t = jnp.concatenate([t, jnp.zeros((LANES, tab.shape[0] - n_ops), F32)], 1)
        tab[:, pl.ds(c * LANES, LANES)] = t.T.astype(BF16)

    lane_at = lax.broadcasted_iota(jnp.int32, (GROUP * per_share, LANES), 1)
    rows_all = n_narrow * n_rows
    spot = lax.broadcasted_iota(jnp.int32, (8, rows_all), 1)
    per_part = 2 * per_chunk
    place_of = (spot // (n_narrow * per_part)) * per_chunk + spot % per_part // 2
    holds = jnp.zeros((8, rows_all), jnp.int32)
    for i, (w, _) in enumerate(peers):
        holds = jnp.where(place_of == i, w, holds)
    holds = spot // per_part % n_narrow * n_rows + holds * 2 + spot % 2
    row_at = [
        jnp.broadcast_to(holds[0:1, t : t + LANES], (GROUP * per_share, LANES))
        for t in range(0, rows_all, LANES)
    ]

    def entries(g, kind):
        here = lists[kind, g]
        columns = [here[:, u : u + 1] for u in range(GROUP)]
        return jnp.concatenate([jnp.broadcast_to(c, (per_share, LANES)) for c in columns], 0)

    def one_hot(index, lanes):
        tiles = [jnp.where(index == at, 1.0, 0.0).astype(BF16) for at in lanes]
        return jnp.concatenate(tiles, 1)

    operators_at = [lane_at + t for t in range(0, tab.shape[0], LANES)]

    def pick_operators(g, c):
        onehot = one_hot(entries(g, 0), operators_at)
        picks[g] = jnp.dot(onehot, tab[...], preferred_element_type=F32)
        return c

    def pick(first, last):
        lax.fori_loop(first, last, pick_operators, 0)

    def block_copy(c, block, to):
        return pltpu.make_async_remote_copy(
            src_ref=x_all.at[c, block], dst_ref=x_all.at[c, block], send_sem=n_ss,
            recv_sem=n_rs.at[c * n_narrow + block], device_id=(me_w, to), device_id_type=MESH)

    def gather_slices(c):
        first = c * per_chunk
        count = per_chunk if c == 0 else per_chunk - 1
        all_of(x_got, x_got, x_ss, x_rs.at[c], first, count).wait_recv()
        x_all[c, me_n] = x_got[first : first + per_chunk].reshape(per_part, 2 * LANES)
        for to in (n_up, n_dn, n_par):
            block_copy(c, me_n, to).start()

    def pass_on(c):
        block_copy(c, n_dn, n_up).wait_recv()
        for to in (n_up, n_cross, n_par):
            block_copy(c, n_dn, to).start()
        block_copy(c, n_up, n_up).wait_recv()
        block_copy(c, n_up, n_par).start()

    gather_slices(1)
    gather_slices(0)
    all_of(list_got, list_got, list_ss, list_rs).wait_recv()
    first = GROUP - n_words
    lane = lax.broadcasted_iota(jnp.int32, (per_share, LANES), 1)
    for h in range(SHARES):
        mine = slice(h * n_wide // SHARES, (h + 1) * n_wide // SHARES)
        for kind in range(2):
            words = list_got[mine, kind, :]
            words = jnp.concatenate([words, pltpu.roll(words, LANES // 2, 1)], 0)
            field = [lax.shift_right_logical(words, 9 * k) & 511 for k in range(FIELDS)]
            early = jnp.where(lane < n_words, field[0], pltpu.roll(field[1], n_words, 1))
            late = jnp.where(lane < n_words, field[2], pltpu.roll(field[1], n_words - first, 1))
            lists[kind, h * STEPS] = early
            lists[kind, h * STEPS + 1] = jnp.where(lane < n_list - GROUP, late, NO_OPERATOR)
    pass_on(1)
    pick(0, 2)
    pass_on(0)
    pick(2, SHARES * STEPS)
    for c in range(CHUNKS):
        for n in (n_far, n_par, n_par + n_up - me_n, n_par + n_dn - me_n, n_par + n_far - me_n):
            block_copy(c, n, n_up).wait_recv()
    pat = x_all[...].astype(BF16).reshape(rows_all, 2 * LANES)

    def translate(g, c):
        onehot = one_hot(entries(g, 1), row_at)
        px = jnp.dot(onehot, pat, preferred_element_type=F32)
        pt = picks[g]
        xr, xi = px[:, :LANES], px[:, LANES:]
        tr, ti = pt[:, :LANES], pt[:, LANES:]
        real = (tr * xr - ti * xi).reshape(GROUP, per_share, LANES).sum(0)
        imag = (tr * xi + ti * xr).reshape(GROUP, per_share, LANES).sum(0)
        return c[0] + real, c[1] + imag

    for h in range(SHARES):
        zero = jnp.zeros((per_share, LANES), F32)
        real, imag = lax.fori_loop(h * STEPS, (h + 1) * STEPS, translate, (zero, zero))
        mine = slice(h * n_wide // SHARES, (h + 1) * n_wide // SHARES)
        for j in range(2):
            rows = slice(j * per_share // 2, (j + 1) * per_share // 2)
            r_send[mine, j, pl.ds(0, LANES)] = real[rows]
            r_send[mine, j, pl.ds(LANES, LANES)] = imag[rows]
        for i in range(mine.start, min(mine.stop, n_wide - 1)):
            slice_copy(r_send, i, r_got, me_w, peers[i][0], r_ss, r_rs).start()
    r_got[me_w] = r_send[n_wide - 1]
    all_of(r_got, r_got, r_ss, r_rs).wait_recv()

    tiles = [None] * (q1 // LANES)
    at = lax.broadcasted_iota(jnp.int32, (4, LANES), 1)
    for w in range(n_wide):
        tile, off = divmod(w * dirs, LANES)
        piece = jnp.concatenate(
            [r_got[w, :, pl.ds(0, LANES)], r_got[w, :, pl.ds(LANES, LANES)]], 0
        )
        if off:
            piece = pltpu.roll(piece, off, 1)
        if tiles[tile] is None:
            tiles[tile] = piece
        else:
            tiles[tile] = jnp.where(at < off, tiles[tile], piece)
        if off + dirs > LANES:
            tiles[tile + 1] = piece
    for i, tile in enumerate(tiles):
        inc[:, pl.ds(i * LANES, LANES)] = tile

    for i in range(parts):
        cols = pl.ds(i * chunk, chunk)
        co = cosv[:, cols]
        si = sinv[:, cols]
        real, imag = [], []
        for p in range(2):
            ir = inc[pl.ds(p, 1), cols]
            ii = inc[pl.ds(2 + p, 1), cols]
            real.append(co * ir + si * ii)
            imag.append(co * ii - si * ir)
        down[:, cols] = jnp.concatenate(real + imag, 0).astype(BF16)
    received = lax.dot_general(
        down[...], itp[...], (((1,), (1,)), ((), ())), preferred_element_type=F32
    ).astype(BF16)

    both = jnp.dot(received, planes[...], preferred_element_type=F32)
    by_real, by_imag = both[:, :n_bases], both[:, n_bases:]
    out_ref[pl.ds(0, boxes), :] = by_real[:boxes] + by_imag[boxes:]
    out_ref[pl.ds(boxes, boxes), :] = by_real[boxes:] - by_imag[:boxes]

    all_of(list_got, list_got, list_ss, list_rs).wait_send()
    all_of(x_send, x_got, x_ss, x_rs.at[0]).wait_send()
    all_of(r_send, r_got, r_ss, r_rs).wait_send()
    for c in range(CHUNKS):
        pltpu.make_async_remote_copy(
            src_ref=x_all.at[c, pl.ds(0, n_narrow - 1)],
            dst_ref=x_all.at[c, pl.ds(0, n_narrow - 1)],
            send_sem=n_ss, recv_sem=n_rs.at[0], device_id=(me_w, n_up), device_id_type=MESH,
        ).wait_send()


def solution(mesh):
    n_wide, n_narrow = mesh.shape["wide"], mesh.shape["narrow"]
    n_z = 8
    both = ("wide", "narrow")

    def on_device(coef, rad, interp, angles, table, sources, operators, counts):
        boxes, _, n_bases = coef.shape
        q0, q1 = interp.shape
        n_ops = table.shape[0]
        n_list = sources.shape[1]
        chunk = 256
        parts = q1 // chunk
        rows = 2 * n_wide
        rad_raw = jnp.transpose(rad, (2, 0, 1))
        table_t = jnp.transpose(table, (1, 2, 0))
        n_tab = -(-n_ops // LANES) * LANES
        assert n_list % FIELDS == 0 and n_list <= GROUP * STEPS
        assert n_list // FIELDS <= LANES // 2
        vmem = pl.BlockSpec(memory_space=pltpu.VMEM)
        anyw = pl.BlockSpec(memory_space=pl.ANY)
        dma = pltpu.SemaphoreType.DMA
        slots = (n_wide, 2, 2 * LANES)
        result = pl.pallas_call(
            functools.partial(kernel, (n_wide, n_narrow, n_z, chunk)),
            out_shape=pltpu.VMEM((2 * boxes, n_bases), F32),
            in_specs=[anyw] * 8,
            out_specs=vmem,
            scratch_shapes=[
                pltpu.SMEM(counts.shape, jnp.int32),
                pltpu.VMEM(coef.shape, BF16),
                pltpu.VMEM(angles.shape, F32),
                pltpu.VMEM(table_t.shape, F32),
                pltpu.VMEM(sources.shape, jnp.int32),
                pltpu.VMEM(operators.shape, jnp.int32),
                pltpu.VMEM((q0, 2, n_bases), BF16),
                pltpu.VMEM((2 * q0, n_bases), BF16),
                pltpu.VMEM((q0, q1), BF16),
                pltpu.VMEM((8, q1), F32),
                pltpu.VMEM((8, q1), F32),
                pltpu.VMEM((n_bases // LANES, 2 * q0, LANES), F32),
                pltpu.VMEM((q0, 2 * n_bases), BF16),
                pltpu.VMEM((n_bases // LANES, 2 * boxes, LANES), F32),
                pltpu.VMEM((4, q1), F32),
                pltpu.VMEM((2, LANES), jnp.int32),
                pltpu.VMEM((n_wide, 2, LANES), jnp.int32),
                pltpu.VMEM((2, SHARES * STEPS, rows // SHARES, LANES), jnp.int32),
                pltpu.VMEM(slots, F32),
                pltpu.VMEM(slots, F32),
                pltpu.VMEM((CHUNKS, n_narrow, rows // CHUNKS, 2 * LANES), F32),
                pltpu.VMEM((n_tab, 2 * LANES), BF16),
                pltpu.VMEM((SHARES * STEPS, GROUP * rows // SHARES, 2 * LANES), F32),
                pltpu.VMEM((2 * boxes, q1), BF16),
                pltpu.VMEM(slots, F32),
                pltpu.VMEM(slots, F32),
                pltpu.VMEM((4, q1), F32),
                dma((parts + 6 + -(-q0 // ROWS),)),
                dma, dma, dma, dma((CHUNKS,)), dma, dma((CHUNKS * n_narrow,)), dma, dma,
            ],
            compiler_params=pltpu.CompilerParams(
                collective_id=0, has_side_effects=True, vmem_limit_bytes=60 * 1024 * 1024
            ),
            name="fmm_step",
        )(counts, coef, rad_raw, interp, angles, table_t, sources, operators)
        return jnp.transpose(result.reshape(2, boxes, n_bases), (1, 0, 2))

    return jax.shard_map(
        on_device,
        mesh=mesh,
        in_specs=(
            P(both, None, None), P(), P(), P(), P(None, None, "wide"),
            P(both, None), P(both, None), P(both),
        ),
        out_specs=P(both, None, None),
        check_vma=False,
    )
```

```python
import functools

import jax
import jax.numpy as jnp
from jax import lax
from jax.experimental import pallas as pl
from jax.experimental.pallas import tpu as pltpu
from jax.sharding import PartitionSpec as P

MESH = pl.DeviceIdType.MESH
BF16 = jnp.bfloat16
F32 = jnp.float32
LANES = 128
GROUP = 96
STEPS = 2
SHARES = 4
NEAR_FROM = 20
ROWS = 112
FIELDS = 3
NO_OPERATOR = 511


def offsets_along(n_x, n_z):
    def hops(o):
        return min(o[0], n_x - o[0]) + min(o[1], n_z - o[1])

    return sorted(((a, b) for a in range(n_x) for b in range(n_z)), key=lambda o: (-hops(o), o))


def kernel(
    dims,
    counts_hbm, coef_hbm, rad_hbm, int_hbm, ang_hbm, tab_hbm, src_hbm, opr_hbm,
    out_ref,
    counts_ref, coef_ref, ang_ref, tab_ref, src_ref, opr_ref,
    raw, rad, itp, cosv, sinv, work, planes, coefs, outg, list_send, list_got, lists, x_send, x_got, x_all,
    tab, picks, down, r_send, r_got, inc,
    mem_sem, list_ss, list_rs, x_ss, x_rs, n_ss, n_rs, r_ss, r_rs,
):
    n_wide, n_narrow, n_z, chunk = dims
    n_x = n_wide // n_z
    me_w = lax.axis_index("wide")
    me_n = lax.axis_index("narrow")
    me_x, me_z = me_w // n_z, me_w % n_z
    q0, q1 = int_hbm.shape
    parts = q1 // chunk
    dirs = q1 // n_wide
    n_list = src_ref.shape[1]
    n_rows = 2 * n_wide
    per_share = n_rows // SHARES
    spans = [(0, NEAR_FROM), (NEAR_FROM, n_wide)]
    boxes = coef_ref.shape[0]

    small = [
        pltpu.make_async_copy(a, b, mem_sem.at[parts + i])
        for i, (a, b) in enumerate([
            (coef_hbm, coef_ref), (src_hbm, src_ref), (opr_hbm, opr_ref),
            (counts_hbm, counts_ref), (ang_hbm, ang_ref), (tab_hbm, tab_ref),
        ])
    ]
    small[0].start()
    blocks = [(q, min(q + ROWS, q0)) for q in range(0, q0, ROWS)]
    rad_copies = [
        pltpu.make_async_copy(rad_hbm.at[a:b], raw.at[a:b], mem_sem.at[parts + 6 + i])
        for i, (a, b) in enumerate(blocks)
    ]
    for copy in rad_copies + small[1:5]:
        copy.start()

    def int_copy(i):
        cols = pl.ds(i * chunk, chunk)
        return pltpu.make_async_copy(int_hbm.at[:, cols], itp.at[:, cols], mem_sem.at[i])

    barrier = pltpu.get_barrier_semaphore()
    offsets = offsets_along(n_x, n_z)
    place = {o: i for i, o in enumerate(offsets)}
    peers = []
    for dx, dz in offsets:
        w = lax.rem(me_x + dx, n_x) * n_z + lax.rem(me_z + dz, n_z)
        peers.append((w, place[(-dx) % n_x, (-dz) % n_z]))
    for w, _ in peers[:-1]:
        pl.semaphore_signal(barrier, 1, device_id=(w, me_n), device_id_type=MESH)
    me_y, me_c = me_n // 2, me_n % 2
    n_y = n_narrow // 2
    ahead = 1 - 2 * me_c
    n_up = lax.rem(me_y + ahead + n_y, n_y) * 2 + me_c
    n_dn = lax.rem(me_y - ahead + n_y, n_y) * 2 + me_c
    n_far = lax.rem(me_y + 2, n_y) * 2 + me_c
    n_par = me_y * 2 + 1 - me_c
    n_cross = n_up + ahead
    for n in (n_up, n_dn, n_par, n_cross):
        pl.semaphore_signal(barrier, 1, device_id=(me_w, n), device_id_type=MESH)

    for i in range(parts):
        int_copy(i).start()
    small[5].start()

    small[0].wait()
    tiled = coef_ref[...].astype(F32).reshape(2 * boxes, -1)
    bases = range(coefs.shape[0])
    for t in bases:
        coefs[t] = tiled[:, t * LANES : (t + 1) * LANES]
    real, imag = [
        jnp.concatenate([coefs[t, pl.ds(c, boxes, stride=2), :] for t in bases], 1)
        for c in range(2)
    ]
    coef = jnp.concatenate(
        [jnp.concatenate([real, -imag], 1), jnp.concatenate([imag, real], 1)], 0
    ).astype(BF16)

    n_bases = rad_hbm.shape[2]
    for copy, (a, b) in zip(rad_copies, blocks):
        copy.wait()
        rows = pl.ds(2 * a, 2 * (b - a))
        rad[rows, :] = raw[a:b].reshape(2 * (b - a), n_bases)
        for t in bases:
            work[t, rows, :] = rad[rows, pl.ds(t * LANES, LANES)].astype(F32)
            for c in range(2):
                planes[pl.ds(a, b - a), pl.ds(c * n_bases + t * LANES, LANES)] = work[
                    t, pl.ds(2 * a + c, b - a, stride=2), :
                ].astype(BF16)
    leaf = lax.dot_general(
        coef, planes[...], (((1,), (1,)), ((), ())), preferred_element_type=F32
    ).astype(BF16)

    def up_chunk(i):
        cols = pl.ds(i * chunk, chunk)
        ang = ang_ref[:, cols]
        co = jnp.cos(ang)
        si = jnp.sin(ang)
        cosv[:, cols] = co
        sinv[:, cols] = si
        up = jnp.dot(leaf, itp[:, cols], preferred_element_type=F32)
        for p in range(2):
            ur = up[8 * p : 8 * p + 8]
            ui = up[boxes + 8 * p : boxes + 8 * p + 8]
            outg[pl.ds(p, 1), cols] = jnp.sum(co * ur - si * ui, 0, keepdims=True)
            outg[pl.ds(2 + p, 1), cols] = jnp.sum(co * ui + si * ur, 0, keepdims=True)

    small[4].wait()
    groups = [(0, 4), (4, 8), (8, 11), (11, parts)]

    def up_group(first, last):
        for i in range(first, last):
            int_copy(i).wait()
        for i in range(first, last):
            up_chunk(i)

    for g in groups[:-1]:
        up_group(*g)

    for copy in small[1:4]:
        copy.wait()
    src = src_ref[...]
    opr = opr_ref[...]
    half = lax.shift_right_logical(src, 1)
    row = (half % n_narrow) * n_rows + (half // n_narrow) * 2 + (src & 1)
    lane = lax.broadcasted_iota(jnp.int32, src.shape, 1)
    which = lax.broadcasted_iota(jnp.int32, src.shape, 0)
    limit = jnp.where(which == 0, counts_ref[0], counts_ref[1])
    wanted = jnp.where(lane < limit, opr, NO_OPERATOR)
    n_words = n_list // FIELDS
    at = lax.broadcasted_iota(jnp.int32, (1, LANES), 1)
    for kind, value in enumerate((wanted, row)):
        value = jnp.concatenate(
            [value, jnp.full((2, 2 * LANES - n_list), NO_OPERATOR, jnp.int32)], 1
        )
        word = jnp.zeros((2, LANES), jnp.int32)
        for k in range(FIELDS):
            word = word + (pltpu.roll(value, (2 * LANES - k * n_words) % (2 * LANES), 1)[:, :LANES] << (9 * k))
        list_send[pl.ds(kind, 1), :] = jnp.where(
            at < LANES // 2, word[0:1], pltpu.roll(word[1:2], LANES // 2, 1)
        )

    up_group(*groups[-1])

    for w in range(n_wide):
        tile, off = divmod(w * dirs, LANES)
        piece = outg[:, pl.ds(tile * LANES, LANES)]
        if off:
            piece = pltpu.roll(piece, LANES - off, 1)
            if off + dirs > LANES:
                more = pltpu.roll(outg[:, pl.ds((tile + 1) * LANES, LANES)], LANES - off, 1)
                at = lax.broadcasted_iota(jnp.int32, piece.shape, 1)
                piece = jnp.where(at < LANES - off, piece, more)
        x_send[w, :, pl.ds(0, LANES)] = piece[0:2]
        x_send[w, :, pl.ds(LANES, LANES)] = piece[2:4]

    def slice_copy(src_all, at, dst_all, there, w, send_sem, recv_sem):
        return pltpu.make_async_remote_copy(
            src_ref=src_all.at[at], dst_ref=dst_all.at[there], send_sem=send_sem,
            recv_sem=recv_sem, device_id=(w, me_n), device_id_type=MESH)

    def all_of(src_all, dst_all, send_sem, recv_sem, first=0, count=n_wide - 1):
        some = pl.ds(first, count)
        return pltpu.make_async_remote_copy(
            src_ref=src_all.at[some], dst_ref=dst_all.at[some], send_sem=send_sem,
            recv_sem=recv_sem, device_id=(peers[0][0], me_n), device_id_type=MESH)

    pl.semaphore_wait(barrier, n_wide - 1 + 4)
    for w, there in peers[:-1]:
        slice_copy(x_send, w, x_got, there, w, x_ss, x_rs.at[int(there >= NEAR_FROM)]).start()
    x_got[n_wide - 1] = x_send[me_w]

    def list_copy(w, there):
        return pltpu.make_async_remote_copy(
            src_ref=list_send, dst_ref=list_got.at[there], send_sem=list_ss, recv_sem=list_rs,
            device_id=(w, me_n), device_id_type=MESH)

    for w, there in peers[:-1]:
        list_copy(w, there).start()
    list_got[n_wide - 1] = list_send[...]


    small[5].wait()
    n_ops = tab_ref.shape[2]
    for c in range(2):
        t = tab_ref[c]
        t = jnp.concatenate([t, jnp.zeros((LANES - dirs, n_ops), F32)], 0)
        t = jnp.concatenate([t, jnp.zeros((LANES, tab.shape[0] - n_ops), F32)], 1)
        tab[:, pl.ds(c * LANES, LANES)] = t.T.astype(BF16)

    lane_at = lax.broadcasted_iota(jnp.int32, (GROUP * per_share, LANES), 1)
    rows_all = n_narrow * n_rows
    spot = lax.broadcasted_iota(jnp.int32, (8, rows_all), 1)
    place_of = spot % n_rows // 2
    holds = jnp.zeros((8, rows_all), jnp.int32)
    for i, (w, _) in enumerate(peers):
        holds = jnp.where(place_of == i, w, holds)
    holds = spot // n_rows * n_rows + holds * 2 + spot % 2
    row_at = [
        jnp.broadcast_to(holds[0:1, t : t + LANES], (GROUP * per_share, LANES))
        for t in range(0, rows_all, LANES)
    ]

    def entries(g, kind):
        here = lists[kind, g]
        columns = [here[:, u : u + 1] for u in range(GROUP)]
        return jnp.concatenate([jnp.broadcast_to(c, (per_share, LANES)) for c in columns], 0)

    def one_hot(index, lanes):
        tiles = [jnp.where(index == at, 1.0, 0.0).astype(BF16) for at in lanes]
        return jnp.concatenate(tiles, 1)

    operators_at = [lane_at + t for t in range(0, tab.shape[0], LANES)]

    def pick_operators(g, c):
        onehot = one_hot(entries(g, 0), operators_at)
        picks[g] = jnp.dot(onehot, tab[...], preferred_element_type=F32)
        return c

    def pick(first, last):
        lax.fori_loop(first, last, pick_operators, 0)

    def rows_of(c):
        first, last = spans[c]
        return pl.ds(2 * first, 2 * (last - first))

    def block_copy(c, block, to):
        return pltpu.make_async_remote_copy(
            src_ref=x_all.at[block, rows_of(c)], dst_ref=x_all.at[block, rows_of(c)], send_sem=n_ss,
            recv_sem=n_rs.at[c * n_narrow + block], device_id=(me_w, to), device_id_type=MESH)

    def gather_slices(c):
        first, last = spans[c]
        count = min(last, n_wide - 1) - first
        all_of(x_got, x_got, x_ss, x_rs.at[c], first, count).wait_recv()
        x_all[me_n, rows_of(c), :] = x_got[first:last].reshape(2 * (last - first), 2 * LANES)
        for to in (n_up, n_dn, n_par):
            block_copy(c, me_n, to).start()

    def pass_on(c):
        block_copy(c, n_dn, n_up).wait_recv()
        for to in (n_up, n_cross, n_par):
            block_copy(c, n_dn, to).start()
        block_copy(c, n_up, n_up).wait_recv()
        block_copy(c, n_up, n_par).start()

    gather_slices(1)
    gather_slices(0)
    all_of(list_got, list_got, list_ss, list_rs).wait_recv()
    first = GROUP - n_words
    lane = lax.broadcasted_iota(jnp.int32, (per_share, LANES), 1)
    for h in range(SHARES):
        mine = slice(h * n_wide // SHARES, (h + 1) * n_wide // SHARES)
        for kind in range(2):
            words = list_got[mine, kind, :]
            words = jnp.concatenate([words, pltpu.roll(words, LANES // 2, 1)], 0)
            field = [lax.shift_right_logical(words, 9 * k) & 511 for k in range(FIELDS)]
            early = jnp.where(lane < n_words, field[0], pltpu.roll(field[1], n_words, 1))
            late = jnp.where(lane < n_words, field[2], pltpu.roll(field[1], n_words - first, 1))
            lists[kind, h * STEPS] = early
            lists[kind, h * STEPS + 1] = jnp.where(lane < n_list - GROUP, late, NO_OPERATOR)
    pass_on(1)
    pick(0, 2)
    pass_on(0)
    pick(2, SHARES * STEPS)
    for c in range(2):
        for n in (n_far, n_par, n_par + n_up - me_n, n_par + n_dn - me_n, n_par + n_far - me_n):
            block_copy(c, n, n_up).wait_recv()
    pat = x_all[...].astype(BF16).reshape(rows_all, 2 * LANES)

    def translate(g, c):
        onehot = one_hot(entries(g, 1), row_at)
        px = jnp.dot(onehot, pat, preferred_element_type=F32)
        pt = picks[g]
        xr, xi = px[:, :LANES], px[:, LANES:]
        tr, ti = pt[:, :LANES], pt[:, LANES:]
        real = (tr * xr - ti * xi).reshape(GROUP, per_share, LANES).sum(0)
        imag = (tr * xi + ti * xr).reshape(GROUP, per_share, LANES).sum(0)
        return c[0] + real, c[1] + imag

    for h in range(SHARES):
        zero = jnp.zeros((per_share, LANES), F32)
        real, imag = lax.fori_loop(h * STEPS, (h + 1) * STEPS, translate, (zero, zero))
        mine = slice(h * n_wide // SHARES, (h + 1) * n_wide // SHARES)
        for j in range(2):
            rows = slice(j * per_share // 2, (j + 1) * per_share // 2)
            r_send[mine, j, pl.ds(0, LANES)] = real[rows]
            r_send[mine, j, pl.ds(LANES, LANES)] = imag[rows]
        for i in range(mine.start, min(mine.stop, n_wide - 1)):
            slice_copy(r_send, i, r_got, me_w, peers[i][0], r_ss, r_rs).start()
    r_got[me_w] = r_send[n_wide - 1]
    all_of(r_got, r_got, r_ss, r_rs).wait_recv()

    tiles = [None] * (q1 // LANES)
    at = lax.broadcasted_iota(jnp.int32, (4, LANES), 1)
    for w in range(n_wide):
        tile, off = divmod(w * dirs, LANES)
        piece = jnp.concatenate(
            [r_got[w, :, pl.ds(0, LANES)], r_got[w, :, pl.ds(LANES, LANES)]], 0
        )
        if off:
            piece = pltpu.roll(piece, off, 1)
        if tiles[tile] is None:
            tiles[tile] = piece
        else:
            tiles[tile] = jnp.where(at < off, tiles[tile], piece)
        if off + dirs > LANES:
            tiles[tile + 1] = piece
    for i, tile in enumerate(tiles):
        inc[:, pl.ds(i * LANES, LANES)] = tile

    for i in range(parts):
        cols = pl.ds(i * chunk, chunk)
        co = cosv[:, cols]
        si = sinv[:, cols]
        real, imag = [], []
        for p in range(2):
            ir = inc[pl.ds(p, 1), cols]
            ii = inc[pl.ds(2 + p, 1), cols]
            real.append(co * ir + si * ii)
            imag.append(co * ii - si * ir)
        down[:, cols] = jnp.concatenate(real + imag, 0).astype(BF16)
    received = lax.dot_general(
        down[...], itp[...], (((1,), (1,)), ((), ())), preferred_element_type=F32
    ).astype(BF16)

    both = jnp.dot(received, planes[...], preferred_element_type=F32)
    by_real, by_imag = both[:, :n_bases], both[:, n_bases:]
    out_ref[pl.ds(0, boxes), :] = by_real[:boxes] + by_imag[boxes:]
    out_ref[pl.ds(boxes, boxes), :] = by_real[boxes:] - by_imag[:boxes]

    all_of(list_got, list_got, list_ss, list_rs).wait_send()
    all_of(x_send, x_got, x_ss, x_rs.at[0]).wait_send()
    all_of(r_send, r_got, r_ss, r_rs).wait_send()
    blocks = pl.ds(0, n_narrow - 1)
    pltpu.make_async_remote_copy(
        src_ref=x_all.at[blocks], dst_ref=x_all.at[blocks], send_sem=n_ss, recv_sem=n_rs.at[0],
        device_id=(me_w, n_up), device_id_type=MESH,
    ).wait_send()


def solution(mesh):
    n_wide, n_narrow = mesh.shape["wide"], mesh.shape["narrow"]
    n_z = 8
    both = ("wide", "narrow")

    def on_device(coef, rad, interp, angles, table, sources, operators, counts):
        boxes, _, n_bases = coef.shape
        q0, q1 = interp.shape
        n_ops = table.shape[0]
        n_list = sources.shape[1]
        chunk = 256
        parts = q1 // chunk
        rows = 2 * n_wide
        rad_raw = jnp.transpose(rad, (2, 0, 1))
        table_t = jnp.transpose(table, (1, 2, 0))
        n_tab = -(-n_ops // LANES) * LANES
        assert n_list % FIELDS == 0 and n_list <= GROUP * STEPS
        assert n_list // FIELDS <= LANES // 2
        vmem = pl.BlockSpec(memory_space=pltpu.VMEM)
        anyw = pl.BlockSpec(memory_space=pl.ANY)
        dma = pltpu.SemaphoreType.DMA
        slots = (n_wide, 2, 2 * LANES)
        result = pl.pallas_call(
            functools.partial(kernel, (n_wide, n_narrow, n_z, chunk)),
            out_shape=pltpu.VMEM((2 * boxes, n_bases), F32),
            in_specs=[anyw] * 8,
            out_specs=vmem,
            scratch_shapes=[
                pltpu.SMEM(counts.shape, jnp.int32),
                pltpu.VMEM(coef.shape, BF16),
                pltpu.VMEM(angles.shape, F32),
                pltpu.VMEM(table_t.shape, F32),
                pltpu.VMEM(sources.shape, jnp.int32),
                pltpu.VMEM(operators.shape, jnp.int32),
                pltpu.VMEM((q0, 2, n_bases), BF16),
                pltpu.VMEM((2 * q0, n_bases), BF16),
                pltpu.VMEM((q0, q1), BF16),
                pltpu.VMEM((8, q1), F32),
                pltpu.VMEM((8, q1), F32),
                pltpu.VMEM((n_bases // LANES, 2 * q0, LANES), F32),
                pltpu.VMEM((q0, 2 * n_bases), BF16),
                pltpu.VMEM((n_bases // LANES, 2 * boxes, LANES), F32),
                pltpu.VMEM((4, q1), F32),
                pltpu.VMEM((2, LANES), jnp.int32),
                pltpu.VMEM((n_wide, 2, LANES), jnp.int32),
                pltpu.VMEM((2, SHARES * STEPS, rows // SHARES, LANES), jnp.int32),
                pltpu.VMEM(slots, F32),
                pltpu.VMEM(slots, F32),
                pltpu.VMEM((n_narrow, rows, 2 * LANES), F32),
                pltpu.VMEM((n_tab, 2 * LANES), BF16),
                pltpu.VMEM((SHARES * STEPS, GROUP * rows // SHARES, 2 * LANES), F32),
                pltpu.VMEM((2 * boxes, q1), BF16),
                pltpu.VMEM(slots, F32),
                pltpu.VMEM(slots, F32),
                pltpu.VMEM((4, q1), F32),
                dma((parts + 6 + -(-q0 // ROWS),)),
                dma, dma, dma, dma((2,)), dma, dma((2 * n_narrow,)), dma, dma,
            ],
            compiler_params=pltpu.CompilerParams(
                collective_id=0, has_side_effects=True, vmem_limit_bytes=60 * 1024 * 1024
            ),
            name="fmm_step",
        )(counts, coef, rad_raw, interp, angles, table_t, sources, operators)
        return jnp.transpose(result.reshape(2, boxes, n_bases), (1, 0, 2))

    return jax.shard_map(
        on_device,
        mesh=mesh,
        in_specs=(
            P(both, None, None), P(), P(), P(), P(None, None, "wide"),
            P(both, None), P(both, None), P(both),
        ),
        out_specs=P(both, None, None),
        check_vma=False,
    )
```

```python
import functools

import jax
import jax.numpy as jnp
from jax import lax
from jax.experimental import pallas as pl
from jax.experimental.pallas import tpu as pltpu
from jax.sharding import PartitionSpec as P

MESH = pl.DeviceIdType.MESH
BF16 = jnp.bfloat16
F32 = jnp.float32
LANES = 128
GROUP = 96
STEPS = 2
SHARES = 4
NEAR_FROM = 20
ROWS = 112
FIELDS = 3
NO_OPERATOR = 511


def offsets_along(n_x, n_z):
    def hops(o):
        return min(o[0], n_x - o[0]) + min(o[1], n_z - o[1])

    return sorted(((a, b) for a in range(n_x) for b in range(n_z)), key=lambda o: (-hops(o), o))


def kernel(
    dims,
    counts_hbm, coef_hbm, rad_hbm, int_hbm, ang_hbm, tab_hbm, src_hbm, opr_hbm,
    out_ref,
    counts_ref, coef_ref, ang_ref, tab_ref, src_ref, opr_ref,
    raw, rad, itp, cosv, sinv, work, planes, coefs, outg, list_send, list_got, lists, x_send, x_got, x_all,
    tab, picks, down, r_send, r_got, inc,
    mem_sem, list_ss, list_rs, x_ss, x_rs, n_ss, n_rs, r_ss, r_rs,
):
    n_wide, n_narrow, n_z, chunk = dims
    n_x = n_wide // n_z
    me_w = lax.axis_index("wide")
    me_n = lax.axis_index("narrow")
    me_x, me_z = me_w // n_z, me_w % n_z
    q0, q1 = int_hbm.shape
    parts = q1 // chunk
    dirs = q1 // n_wide
    n_list = src_ref.shape[1]
    n_rows = 2 * n_wide
    per_share = n_rows // SHARES
    spans = [(0, NEAR_FROM), (NEAR_FROM, n_wide)]
    boxes = coef_ref.shape[0]

    small = [
        pltpu.make_async_copy(a, b, mem_sem.at[parts + i])
        for i, (a, b) in enumerate([
            (coef_hbm, coef_ref), (src_hbm, src_ref), (opr_hbm, opr_ref),
            (counts_hbm, counts_ref), (ang_hbm, ang_ref), (tab_hbm, tab_ref),
        ])
    ]
    small[0].start()
    blocks = [(q, min(q + ROWS, q0)) for q in range(0, q0, ROWS)]
    rad_copies = [
        pltpu.make_async_copy(rad_hbm.at[a:b], raw.at[a:b], mem_sem.at[parts + 6 + i])
        for i, (a, b) in enumerate(blocks)
    ]
    for copy in rad_copies + small[1:5]:
        copy.start()

    def int_copy(i):
        cols = pl.ds(i * chunk, chunk)
        return pltpu.make_async_copy(int_hbm.at[:, cols], itp.at[:, cols], mem_sem.at[i])

    barrier = pltpu.get_barrier_semaphore()
    offsets = offsets_along(n_x, n_z)
    place = {o: i for i, o in enumerate(offsets)}
    peers = []
    for dx, dz in offsets:
        w = lax.rem(me_x + dx, n_x) * n_z + lax.rem(me_z + dz, n_z)
        peers.append((w, place[(-dx) % n_x, (-dz) % n_z]))
    for w, _ in peers[:-1]:
        pl.semaphore_signal(barrier, 1, device_id=(w, me_n), device_id_type=MESH)
    me_y, me_c = me_n // 2, me_n % 2
    n_y = n_narrow // 2
    ahead = 1 - 2 * me_c
    n_up = lax.rem(me_y + ahead + n_y, n_y) * 2 + me_c
    n_dn = lax.rem(me_y - ahead + n_y, n_y) * 2 + me_c
    n_far = lax.rem(me_y + 2, n_y) * 2 + me_c
    n_par = me_y * 2 + 1 - me_c
    n_cross = n_up + ahead
    for n in (n_up, n_dn, n_par, n_cross):
        pl.semaphore_signal(barrier, 1, device_id=(me_w, n), device_id_type=MESH)

    for i in range(parts):
        int_copy(i).start()
    small[5].start()

    small[0].wait()
    tiled = coef_ref[...].astype(F32).reshape(2 * boxes, -1)
    bases = range(coefs.shape[0])
    for t in bases:
        coefs[t] = tiled[:, t * LANES : (t + 1) * LANES]
    real, imag = [
        jnp.concatenate([coefs[t, pl.ds(c, boxes, stride=2), :] for t in bases], 1)
        for c in range(2)
    ]
    coef = jnp.concatenate(
        [jnp.concatenate([real, -imag], 1), jnp.concatenate([imag, real], 1)], 0
    ).astype(BF16)

    n_bases = rad_hbm.shape[2]
    for copy, (a, b) in zip(rad_copies, blocks):
        copy.wait()
        rows = pl.ds(2 * a, 2 * (b - a))
        rad[rows, :] = raw[a:b].reshape(2 * (b - a), n_bases)
        for t in bases:
            work[t, rows, :] = rad[rows, pl.ds(t * LANES, LANES)].astype(F32)
            for c in range(2):
                planes[pl.ds(a, b - a), pl.ds(c * n_bases + t * LANES, LANES)] = work[
                    t, pl.ds(2 * a + c, b - a, stride=2), :
                ].astype(BF16)
    leaf = lax.dot_general(
        coef, planes[...], (((1,), (1,)), ((), ())), preferred_element_type=F32
    ).astype(BF16)

    def up_chunk(i):
        cols = pl.ds(i * chunk, chunk)
        ang = ang_ref[:, cols]
        co = jnp.cos(ang)
        si = jnp.sin(ang)
        cosv[:, cols] = co
        sinv[:, cols] = si
        up = jnp.dot(leaf, itp[:, cols], preferred_element_type=F32)
        for p in range(2):
            ur = up[8 * p : 8 * p + 8]
            ui = up[boxes + 8 * p : boxes + 8 * p + 8]
            outg[pl.ds(p, 1), cols] = jnp.sum(co * ur - si * ui, 0, keepdims=True)
            outg[pl.ds(2 + p, 1), cols] = jnp.sum(co * ui + si * ur, 0, keepdims=True)

    small[4].wait()
    groups = [(0, 4), (4, 8), (8, 11), (11, parts)]

    def up_group(first, last):
        for i in range(first, last):
            int_copy(i).wait()
        for i in range(first, last):
            up_chunk(i)

    for g in groups[:-1]:
        up_group(*g)

    for copy in small[1:4]:
        copy.wait()
    src = src_ref[...]
    opr = opr_ref[...]
    half = lax.shift_right_logical(src, 1)
    row = (half % n_narrow) * n_rows + (half // n_narrow) * 2 + (src & 1)
    lane = lax.broadcasted_iota(jnp.int32, src.shape, 1)
    which = lax.broadcasted_iota(jnp.int32, src.shape, 0)
    limit = jnp.where(which == 0, counts_ref[0], counts_ref[1])
    wanted = jnp.where(lane < limit, opr, NO_OPERATOR)
    n_words = n_list // FIELDS
    at = lax.broadcasted_iota(jnp.int32, (1, LANES), 1)
    for kind, value in enumerate((wanted, row)):
        value = jnp.concatenate(
            [value, jnp.full((2, 2 * LANES - n_list), NO_OPERATOR, jnp.int32)], 1
        )
        word = jnp.zeros((2, LANES), jnp.int32)
        for k in range(FIELDS):
            word = word + (pltpu.roll(value, (2 * LANES - k * n_words) % (2 * LANES), 1)[:, :LANES] << (9 * k))
        list_send[pl.ds(kind, 1), :] = jnp.where(
            at < LANES // 2, word[0:1], pltpu.roll(word[1:2], LANES // 2, 1)
        )

    up_group(*groups[-1])

    for w in range(n_wide):
        tile, off = divmod(w * dirs, LANES)
        piece = outg[:, pl.ds(tile * LANES, LANES)]
        if off:
            piece = pltpu.roll(piece, LANES - off, 1)
            if off + dirs > LANES:
                more = pltpu.roll(outg[:, pl.ds((tile + 1) * LANES, LANES)], LANES - off, 1)
                at = lax.broadcasted_iota(jnp.int32, piece.shape, 1)
                piece = jnp.where(at < LANES - off, piece, more)
        x_send[w, :, pl.ds(0, LANES)] = piece[0:2]
        x_send[w, :, pl.ds(LANES, LANES)] = piece[2:4]

    def slice_copy(src_all, at, dst_all, there, w, send_sem, recv_sem):
        return pltpu.make_async_remote_copy(
            src_ref=src_all.at[at], dst_ref=dst_all.at[there], send_sem=send_sem,
            recv_sem=recv_sem, device_id=(w, me_n), device_id_type=MESH)

    def all_of(src_all, dst_all, send_sem, recv_sem, first=0, count=n_wide - 1):
        some = pl.ds(first, count)
        return pltpu.make_async_remote_copy(
            src_ref=src_all.at[some], dst_ref=dst_all.at[some], send_sem=send_sem,
            recv_sem=recv_sem, device_id=(peers[0][0], me_n), device_id_type=MESH)

    pl.semaphore_wait(barrier, n_wide - 1 + 4)
    for w, there in peers[:-1]:
        slice_copy(x_send, w, x_got, there, w, x_ss, x_rs.at[int(there >= NEAR_FROM)]).start()
    x_got[n_wide - 1] = x_send[me_w]

    def list_copy(w, there):
        return pltpu.make_async_remote_copy(
            src_ref=list_send, dst_ref=list_got.at[there], send_sem=list_ss, recv_sem=list_rs,
            device_id=(w, me_n), device_id_type=MESH)

    for w, there in peers[:-1]:
        list_copy(w, there).start()
    list_got[n_wide - 1] = list_send[...]


    small[5].wait()
    n_ops = tab_ref.shape[2]
    for c in range(2):
        t = tab_ref[c]
        t = jnp.concatenate([t, jnp.zeros((LANES - dirs, n_ops), F32)], 0)
        t = jnp.concatenate([t, jnp.zeros((LANES, tab.shape[0] - n_ops), F32)], 1)
        tab[:, pl.ds(c * LANES, LANES)] = t.T.astype(BF16)

    lane_at = lax.broadcasted_iota(jnp.int32, (GROUP * per_share, LANES), 1)
    rows_all = n_narrow * n_rows
    spot = lax.broadcasted_iota(jnp.int32, (8, rows_all), 1)
    place_of = spot % n_rows // 2
    holds = jnp.zeros((8, rows_all), jnp.int32)
    for i, (w, _) in enumerate(peers):
        holds = jnp.where(place_of == i, w, holds)
    holds = spot // n_rows * n_rows + holds * 2 + spot % 2
    row_at = [
        jnp.broadcast_to(holds[0:1, t : t + LANES], (GROUP * per_share, LANES))
        for t in range(0, rows_all, LANES)
    ]

    def entries(g, kind):
        here = lists[kind, g]
        columns = [here[:, u : u + 1] for u in range(GROUP)]
        return jnp.concatenate([jnp.broadcast_to(c, (per_share, LANES)) for c in columns], 0)

    def one_hot(index, lanes):
        tiles = [jnp.where(index == at, 1.0, 0.0).astype(BF16) for at in lanes]
        return jnp.concatenate(tiles, 1)

    operators_at = [lane_at + t for t in range(0, tab.shape[0], LANES)]

    def pick_operators(g, c):
        onehot = one_hot(entries(g, 0), operators_at)
        picks[g] = jnp.dot(onehot, tab[...], preferred_element_type=F32)
        return c

    def pick(first, last):
        lax.fori_loop(first, last, pick_operators, 0, unroll=2 if last - first > 2 else 1)

    def rows_of(c):
        first, last = spans[c]
        return pl.ds(2 * first, 2 * (last - first))

    def block_copy(c, block, to):
        return pltpu.make_async_remote_copy(
            src_ref=x_all.at[block, rows_of(c)], dst_ref=x_all.at[block, rows_of(c)], send_sem=n_ss,
            recv_sem=n_rs.at[c * n_narrow + block], device_id=(me_w, to), device_id_type=MESH)

    def gather_slices(c):
        first, last = spans[c]
        count = min(last, n_wide - 1) - first
        all_of(x_got, x_got, x_ss, x_rs.at[c], first, count).wait_recv()
        x_all[me_n, rows_of(c), :] = x_got[first:last].reshape(2 * (last - first), 2 * LANES)
        for to in (n_up, n_dn, n_par):
            block_copy(c, me_n, to).start()

    def pass_on(c):
        block_copy(c, n_dn, n_up).wait_recv()
        for to in (n_up, n_cross, n_par):
            block_copy(c, n_dn, to).start()
        block_copy(c, n_up, n_up).wait_recv()
        block_copy(c, n_up, n_par).start()

    gather_slices(1)
    gather_slices(0)
    all_of(list_got, list_got, list_ss, list_rs).wait_recv()
    first = GROUP - n_words
    lane = lax.broadcasted_iota(jnp.int32, (per_share, LANES), 1)
    for h in range(SHARES):
        mine = slice(h * n_wide // SHARES, (h + 1) * n_wide // SHARES)
        for kind in range(2):
            words = list_got[mine, kind, :]
            words = jnp.concatenate([words, pltpu.roll(words, LANES // 2, 1)], 0)
            field = [lax.shift_right_logical(words, 9 * k) & 511 for k in range(FIELDS)]
            early = jnp.where(lane < n_words, field[0], pltpu.roll(field[1], n_words, 1))
            late = jnp.where(lane < n_words, field[2], pltpu.roll(field[1], n_words - first, 1))
            lists[kind, h * STEPS] = early
            lists[kind, h * STEPS + 1] = jnp.where(lane < n_list - GROUP, late, NO_OPERATOR)
    pass_on(1)
    pick(0, 2)
    pass_on(0)
    pick(2, SHARES * STEPS)
    for c in range(2):
        for n in (n_far, n_par, n_par + n_up - me_n, n_par + n_dn - me_n, n_par + n_far - me_n):
            block_copy(c, n, n_up).wait_recv()
    pat = x_all[...].astype(BF16).reshape(rows_all, 2 * LANES)

    def translate(g, c):
        onehot = one_hot(entries(g, 1), row_at)
        px = jnp.dot(onehot, pat, preferred_element_type=F32)
        pt = picks[g]
        xr, xi = px[:, :LANES], px[:, LANES:]
        tr, ti = pt[:, :LANES], pt[:, LANES:]
        real = (tr * xr - ti * xi).reshape(GROUP, per_share, LANES).sum(0)
        imag = (tr * xi + ti * xr).reshape(GROUP, per_share, LANES).sum(0)
        return c[0] + real, c[1] + imag

    for h in range(SHARES):
        zero = jnp.zeros((per_share, LANES), F32)
        real, imag = lax.fori_loop(h * STEPS, (h + 1) * STEPS, translate, (zero, zero))
        mine = slice(h * n_wide // SHARES, (h + 1) * n_wide // SHARES)
        for j in range(2):
            rows = slice(j * per_share // 2, (j + 1) * per_share // 2)
            r_send[mine, j, pl.ds(0, LANES)] = real[rows]
            r_send[mine, j, pl.ds(LANES, LANES)] = imag[rows]
        for i in range(mine.start, min(mine.stop, n_wide - 1)):
            slice_copy(r_send, i, r_got, me_w, peers[i][0], r_ss, r_rs).start()
    r_got[me_w] = r_send[n_wide - 1]
    all_of(r_got, r_got, r_ss, r_rs).wait_recv()

    tiles = [None] * (q1 // LANES)
    at = lax.broadcasted_iota(jnp.int32, (4, LANES), 1)
    for w in range(n_wide):
        tile, off = divmod(w * dirs, LANES)
        piece = jnp.concatenate(
            [r_got[w, :, pl.ds(0, LANES)], r_got[w, :, pl.ds(LANES, LANES)]], 0
        )
        if off:
            piece = pltpu.roll(piece, off, 1)
        if tiles[tile] is None:
            tiles[tile] = piece
        else:
            tiles[tile] = jnp.where(at < off, tiles[tile], piece)
        if off + dirs > LANES:
            tiles[tile + 1] = piece
    for i, tile in enumerate(tiles):
        inc[:, pl.ds(i * LANES, LANES)] = tile

    for i in range(parts):
        cols = pl.ds(i * chunk, chunk)
        co = cosv[:, cols]
        si = sinv[:, cols]
        real, imag = [], []
        for p in range(2):
            ir = inc[pl.ds(p, 1), cols]
            ii = inc[pl.ds(2 + p, 1), cols]
            real.append(co * ir + si * ii)
            imag.append(co * ii - si * ir)
        down[:, cols] = jnp.concatenate(real + imag, 0).astype(BF16)
    received = lax.dot_general(
        down[...], itp[...], (((1,), (1,)), ((), ())), preferred_element_type=F32
    ).astype(BF16)

    both = jnp.dot(received, planes[...], preferred_element_type=F32)
    by_real, by_imag = both[:, :n_bases], both[:, n_bases:]
    out_ref[pl.ds(0, boxes), :] = by_real[:boxes] + by_imag[boxes:]
    out_ref[pl.ds(boxes, boxes), :] = by_real[boxes:] - by_imag[:boxes]

    all_of(list_got, list_got, list_ss, list_rs).wait_send()
    all_of(x_send, x_got, x_ss, x_rs.at[0]).wait_send()
    all_of(r_send, r_got, r_ss, r_rs).wait_send()
    blocks = pl.ds(0, n_narrow - 1)
    pltpu.make_async_remote_copy(
        src_ref=x_all.at[blocks], dst_ref=x_all.at[blocks], send_sem=n_ss, recv_sem=n_rs.at[0],
        device_id=(me_w, n_up), device_id_type=MESH,
    ).wait_send()


def solution(mesh):
    n_wide, n_narrow = mesh.shape["wide"], mesh.shape["narrow"]
    n_z = 8
    both = ("wide", "narrow")

    def on_device(coef, rad, interp, angles, table, sources, operators, counts):
        boxes, _, n_bases = coef.shape
        q0, q1 = interp.shape
        n_ops = table.shape[0]
        n_list = sources.shape[1]
        chunk = 256
        parts = q1 // chunk
        rows = 2 * n_wide
        rad_raw = jnp.transpose(rad, (2, 0, 1))
        table_t = jnp.transpose(table, (1, 2, 0))
        n_tab = -(-n_ops // LANES) * LANES
        assert n_list % FIELDS == 0 and n_list <= GROUP * STEPS
        assert n_list // FIELDS <= LANES // 2
        vmem = pl.BlockSpec(memory_space=pltpu.VMEM)
        anyw = pl.BlockSpec(memory_space=pl.ANY)
        dma = pltpu.SemaphoreType.DMA
        slots = (n_wide, 2, 2 * LANES)
        result = pl.pallas_call(
            functools.partial(kernel, (n_wide, n_narrow, n_z, chunk)),
            out_shape=pltpu.VMEM((2 * boxes, n_bases), F32),
            in_specs=[anyw] * 8,
            out_specs=vmem,
            scratch_shapes=[
                pltpu.SMEM(counts.shape, jnp.int32),
                pltpu.VMEM(coef.shape, BF16),
                pltpu.VMEM(angles.shape, F32),
                pltpu.VMEM(table_t.shape, F32),
                pltpu.VMEM(sources.shape, jnp.int32),
                pltpu.VMEM(operators.shape, jnp.int32),
                pltpu.VMEM((q0, 2, n_bases), BF16),
                pltpu.VMEM((2 * q0, n_bases), BF16),
                pltpu.VMEM((q0, q1), BF16),
                pltpu.VMEM((8, q1), F32),
                pltpu.VMEM((8, q1), F32),
                pltpu.VMEM((n_bases // LANES, 2 * q0, LANES), F32),
                pltpu.VMEM((q0, 2 * n_bases), BF16),
                pltpu.VMEM((n_bases // LANES, 2 * boxes, LANES), F32),
                pltpu.VMEM((4, q1), F32),
                pltpu.VMEM((2, LANES), jnp.int32),
                pltpu.VMEM((n_wide, 2, LANES), jnp.int32),
                pltpu.VMEM((2, SHARES * STEPS, rows // SHARES, LANES), jnp.int32),
                pltpu.VMEM(slots, F32),
                pltpu.VMEM(slots, F32),
                pltpu.VMEM((n_narrow, rows, 2 * LANES), F32),
                pltpu.VMEM((n_tab, 2 * LANES), BF16),
                pltpu.VMEM((SHARES * STEPS, GROUP * rows // SHARES, 2 * LANES), F32),
                pltpu.VMEM((2 * boxes, q1), BF16),
                pltpu.VMEM(slots, F32),
                pltpu.VMEM(slots, F32),
                pltpu.VMEM((4, q1), F32),
                dma((parts + 6 + -(-q0 // ROWS),)),
                dma, dma, dma, dma((2,)), dma, dma((2 * n_narrow,)), dma, dma,
            ],
            compiler_params=pltpu.CompilerParams(
                collective_id=0, has_side_effects=True, vmem_limit_bytes=60 * 1024 * 1024
            ),
            name="fmm_step",
        )(counts, coef, rad_raw, interp, angles, table_t, sources, operators)
        return jnp.transpose(result.reshape(2, boxes, n_bases), (1, 0, 2))

    return jax.shard_map(
        on_device,
        mesh=mesh,
        in_specs=(
            P(both, None, None), P(), P(), P(), P(None, None, "wide"),
            P(both, None), P(both, None), P(both),
        ),
        out_specs=P(both, None, None),
        check_vma=False,
    )
```
